32 devices in a mesh: row: 4 (over z), col: 8 (over y, x, core).
Axes of the slice: x: 2, y: 2, z: 4, core: 2. Of those that a mesh axis runs over, the one named last changes fastest.
Arguments:
- resistance: float32 [768, 1024], P('row', 'col'), may hold values from 1 to 100
- ground: float32 [768, 1024], P('row', 'col'), may hold values from 0.001 to 0.01
- nodata: int32 [768, 1024], P('row', 'col'), may hold values 0 or 1
- patch_ids: int32 [768, 1024], P('row', 'col'), may hold values from 0 to 8
Outputs:
- correction: float32 [8, 768, 1024], P(None, 'row', 'col')
The draws below stay inside these ranges and needn't reach their ends.
All inputs are finite; a program needn't handle non-finite values. No bound on the sum of `nodata` on one device may be relied on, other than what follows from the above.
Results may differ from the reference program's by a relative error of at most 0.0003.
Values sent between devices are 32-bit elements; how exact they have to be, the bound alone decides.
No kernel may reach another device: no remote copies, remote signals or barrier semaphores. Data moves between devices by JAX's collectives and lax.ppermute only.
A program may use at most 128 MiB of HBM per device.

```python
import math
import jax
import jax.numpy as jnp
from jax import lax

RHS = 8
ITERS = 4
NR = 768
NC = 1024


def touch_ends(result, key, low, top_value):
    longest = result.shape.index(max(result.shape))
    spots = []
    for shift in (0, 1):
        where = [jax.random.randint(jax.random.fold_in(key, axis), (), 0, length) for axis, length in enumerate(result.shape)]
        where[longest] = (where[longest] + shift) % result.shape[longest]
        spots.append(tuple(where))
    return result.at[spots[0]].set(low).at[spots[1]].set(top_value)


def steps_of(rng, shape, split, least, top_value):
    level = 1.0
    for dim, shards_of in split:
        steps = jax.random.uniform(jax.random.fold_in(jax.random.fold_in(rng, 6), dim), (shards_of,), jnp.float32, least / len(split), top_value / len(split))
        level = level * jnp.repeat(jnp.exp(steps), shape[dim] // shards_of).reshape((-1,) + (1,) * (len(shape) - 1 - dim))
    return level


def setup_inputs(seed: int = 0) -> dict:
    keys = jax.random.split(jax.random.key(seed), 5)
    resistance = jnp.clip(jnp.exp(math.log(100.0) - 4.6051702 * jax.random.uniform(keys[0], (NR, NC), jnp.float32) ** steps_of(keys[0], (NR, NC), ((0, 4), (1, 8)), -0.2, 0.2)), 1.0, 100.0)
    ground = jnp.clip(jnp.exp(math.log(0.01) - 2.30258502 * jax.random.uniform(keys[1], (NR, NC), jnp.float32) ** steps_of(keys[1], (NR, NC), ((0, 4), (1, 8)), -0.2, 0.2)), 0.001, 0.01)
    nodata = touch_ends((jax.random.randint(keys[2], (NR, NC), 0, 10) < 1).astype(jnp.int32), jax.random.fold_in(keys[2], 1), 0, 1)
    patch_ids = touch_ends(jax.random.randint(keys[3], (NR, NC), 0, 9), jax.random.fold_in(keys[3], 1), 0, 8).astype(jnp.int32)
    return {"resistance": resistance, "ground": ground, "nodata": nodata, "patch_ids": patch_ids}


OMEGA = 0.8


def conductance(resist, validity, near_resist, near_valid):
    return (validity * near_valid) * (2.0 / (resist + near_resist))


def edge_terms(res_pad, val_pad):
    resist = res_pad[1:-1, 1:-1]
    validity = val_pad[1:-1, 1:-1]
    north_link = conductance(resist, validity, res_pad[:-2, 1:-1], val_pad[:-2, 1:-1])
    south_link = conductance(resist, validity, res_pad[2:, 1:-1], val_pad[2:, 1:-1])
    west_link = conductance(resist, validity, res_pad[1:-1, :-2], val_pad[1:-1, :-2])
    east_link = conductance(resist, validity, res_pad[1:-1, 2:], val_pad[1:-1, 2:])
    return north_link, south_link, west_link, east_link


def diagonal_of(coeffs):
    return coeffs[0] + coeffs[1] + coeffs[2] + coeffs[3] + coeffs[4]


def apply_operator(values, coeffs, sides):
    above_cells, below_cells, left_cells, right_cells = sides
    pulled = coeffs[1] * above_cells + coeffs[2] * below_cells + coeffs[3] * left_cells + coeffs[4] * right_cells
    return diagonal_of(coeffs) * values - pulled


def restrict_field(values):
    count, rows_here, cols_here = values.shape
    return values.reshape(count, rows_here // 2, 2, cols_here // 2, 2).sum(axis=(2, 4))


def coarse_coeffs(coeffs):
    count, rows_here, cols_here = coeffs.shape
    blocks = coeffs.reshape(count, rows_here // 2, 2, cols_here // 2, 2)
    leakage = blocks[0].sum(axis=(1, 3))
    north_link = blocks[1][:, 0].sum(axis=-1)
    south_link = blocks[2][:, 1].sum(axis=-1)
    west_link = blocks[3][:, :, :, 0].sum(axis=1)
    east_link = blocks[4][:, :, :, 1].sum(axis=1)
    return jnp.stack([leakage, north_link, south_link, west_link, east_link])


def prolong(values):
    return jnp.repeat(jnp.repeat(values, 2, axis=1), 2, axis=2)


def padded_sides(values):
    padded = jnp.pad(values, ((0, 0), (1, 1), (1, 1)))
    return (padded[:, :-2, 1:-1], padded[:, 2:, 1:-1], padded[:, 1:-1, :-2], padded[:, 1:-1, 2:])


def descend(residual, coeffs):
    smoothed = OMEGA * residual / diagonal_of(coeffs)
    remainder = residual - apply_operator(smoothed, coeffs, padded_sides(smoothed))
    return smoothed, restrict_field(remainder)


def reference(resistance, ground, nodata, patch_ids):
    validity = (nodata == 0).astype(jnp.float32)
    res_pad = jnp.pad(resistance, 1)
    val_pad = jnp.pad(validity, 1)
    coeffs = jnp.stack([ground] + list(edge_terms(res_pad, val_pad)))
    coeff_levels = [coeffs]
    for level_no in range(4):
        coeff_levels.append(coarse_coeffs(coeff_levels[-1]))

    def one_source(source):
        residual = validity * ((patch_ids == source + 1).astype(jnp.float32) - 0.125 * (patch_ids > 0).astype(jnp.float32))
        residual = residual[None]
        smooth_list = []
        for level_no in range(4):
            smoothed, residual = descend(residual, coeff_levels[level_no])
            smooth_list.append(smoothed)
        coeffs_last = coeff_levels[4]
        solution = jnp.zeros_like(residual)
        direction = residual
        norm_now = jnp.sum(residual * residual)
        for sweep in range(ITERS):
            image = apply_operator(direction, coeffs_last, padded_sides(direction))
            step_size = norm_now / jnp.sum(direction * image)
            solution = solution + step_size * direction
            residual = residual - step_size * image
            norm_next = jnp.sum(residual * residual)
            direction = residual + (norm_next / norm_now) * direction
            norm_now = norm_next
        upward = solution
        for level_no in reversed(range(4)):
            upward = smooth_list[level_no] + prolong(upward)
        return upward[0]

    return lax.map(one_source, jnp.arange(RHS, dtype=jnp.int32))
```

```python
import functools

import jax
import jax.numpy as jnp
from jax import lax
from jax.experimental import pallas as pl
from jax.experimental.pallas import tpu as pltpu
from jax.sharding import PartitionSpec as P

RHS = 8
ITERS = 4
OMEGA = 0.8
HALO = 16
LANES = 128
F32 = jnp.float32
BF16 = jnp.bfloat16
PIECES = 3


def iota(shape, dim):
    return lax.broadcasted_iota(jnp.int32, shape, dim)


def selection(rows, test):
    shape = (rows, LANES)
    return jnp.where(test(iota(shape, 0), iota(shape, 1)), 1.0, 0.0).astype(BF16)


def dot01(values, matrix, pieces=PIECES):
    total = None
    for piece in range(pieces):
        part = values.astype(BF16)
        term = jnp.dot(part, matrix, preferred_element_type=F32)
        total = term if total is None else total + term
        if piece + 1 < pieces:
            values = values - part.astype(F32)
    return total


def rot(values, shift, axis):
    return pltpu.roll(values, shift % values.shape[axis], axis)


def lanes_of(values, lane):
    return iota(values.shape, 1) if lane is None else lane


def pack_rows_kernel(res_ref, ground_ref, nodata_ref, patch_ref, down_ref, up_ref):
    rows = res_ref.shape[0]
    for out_ref, start in ((down_ref, rows - HALO), (up_ref, 0)):
        part = pl.ds(start, HALO)
        out_ref[0:HALO] = res_ref[part]
        out_ref[HALO : 2 * HALO] = ground_ref[part]
        out_ref[2 * HALO : 3 * HALO] = jnp.where(nodata_ref[part] == 0, 1.0, 0.0)
        out_ref[3 * HALO : 4 * HALO] = patch_ref[part].astype(F32)


def tall_halves(own_refs, above_ref, below_ref):
    res_ref, ground_ref, nodata_ref, patch_ref = own_refs
    own = [
        res_ref[...],
        ground_ref[...],
        jnp.where(nodata_ref[...] == 0, 1.0, 0.0),
        patch_ref[...].astype(F32),
    ]
    half = own[0].shape[0] // 2
    tall = []
    for which, values in enumerate(own):
        part = pl.ds(which * HALO, HALO)
        tall.append(
            (
                jnp.concatenate([above_ref[part], values[:half]], axis=0),
                jnp.concatenate([values[half:], below_ref[part]], axis=0),
            )
        )
    return tall


def pack_cols_kernel(res_ref, ground_ref, nodata_ref, patch_ref, above_ref, below_ref, right_ref, left_ref):
    tall = tall_halves((res_ref, ground_ref, nodata_ref, patch_ref), above_ref, below_ref)
    shape = right_ref.shape
    group_of = iota(shape, 1) // HALO
    to_right = jnp.zeros(shape, F32)
    to_left = jnp.zeros(shape, F32)
    for which in range(4):
        for side in range(2):
            group = 2 * which + side
            values = tall[which][side]
            here = group_of == group
            to_right = jnp.where(here, rot(values, HALO * group + HALO, 1), to_right)
            to_left = jnp.where(here, rot(values, HALO * group, 1), to_left)
    right_ref[...] = to_right
    left_ref[...] = to_left


def link(resist, validity, near_resist, near_valid):
    return (validity * near_valid) * (2.0 / (resist + near_resist))


def weights_of(diag):
    return OMEGA / jnp.where(diag > 0, diag, 1.0)


def down_kernel(
    res_ref,
    ground_ref,
    nodata_ref,
    patch_ref,
    above_ref,
    below_ref,
    left_ref,
    right_ref,
    payload_ref,
    t1_ref,
    w0_ref,
    ext_ref,
    r1_ref,
    r2_ref,
    r3_ref,
    c1_ref,
    c2_ref,
    c3_ref,
    t3_ref,
    t2_ref,
):
    devices = payload_ref.shape[0]
    tall = tall_halves((res_ref, ground_ref, nodata_ref, patch_ref), above_ref, below_ref)
    quarter = tall[0][0].shape[0]
    lane = iota((quarter, LANES), 1)
    from_left = left_ref[...]
    from_right = right_ref[...]
    for which in range(4):
        for side in range(2):
            group = 2 * which + side
            moved = rot(tall[which][side], HALO, 1)
            tile0 = jnp.where(lane < HALO, rot(from_left, -HALO * group, 1), moved)
            tile1 = jnp.where(
                lane < HALO,
                moved,
                jnp.where(lane < 2 * HALO, rot(from_right, HALO - HALO * group, 1), 0.0),
            )
            if which < 2:
                tile0 = jnp.where(tile0 > 0, tile0, 1.0)
                tile1 = jnp.where(tile1 > 0, tile1, 1.0)
            ext_ref[2 * which, pl.ds(side * quarter, quarter), :] = tile0
            ext_ref[2 * which + 1, pl.ds(side * quarter, quarter), :] = tile1

    n1 = quarter
    odd = lane % 2 == 1

    def parity(which, start):
        return [ext_ref[2 * which + tile, pl.ds(start, n1, stride=2), :] for tile in range(2)]

    res_e, res_o = parity(0, 0), parity(0, 1)
    g_e, g_o = parity(1, 0), parity(1, 1)
    v_e, v_o = parity(2, 0), parity(2, 1)
    p_e, p_o = parity(3, 0), parity(3, 1)

    def left_of(pair):
        first, second = rot(pair[0], 1, 1), rot(pair[1], 1, 1)
        return [first, jnp.where(lane == 0, first, second)]

    def right_of(pair):
        first, second = rot(pair[0], -1, 1), rot(pair[1], -1, 1)
        return [jnp.where(lane == LANES - 1, second, first), second]

    west = {}
    for name, res, val in (("e", res_e, v_e), ("o", res_o, v_o)):
        near_res, near_val = left_of(res), left_of(val)
        west[name] = [link(res[t], val[t], near_res[t], near_val[t]) for t in range(2)]
    east = {name: right_of(pair) for name, pair in west.items()}
    level = []
    coarse = []
    for t in range(2):
        v_in = link(res_e[t], v_e[t], res_o[t], v_o[t])
        v_up = link(res_e[t], v_e[t], rot(res_o[t], 1, 0), rot(v_o[t], 1, 0))
        v_dn = rot(v_up, -1, 0)
        we, wo, ee, eo = west["e"][t], west["o"][t], east["e"][t], east["o"][t]
        w_e = weights_of(g_e[t] + v_up + v_in + we + ee)
        w_o = weights_of(g_o[t] + v_in + v_dn + wo + eo)
        a_e = (1.0 - OMEGA) * v_e[t] + w_e * (v_in + jnp.where(odd, we, ee))
        a_o = (1.0 - OMEGA) * v_o[t] + w_o * (v_in + jnp.where(odd, wo, eo))
        b_e = w_e * jnp.where(odd, ee, we)
        b_o = w_o * jnp.where(odd, eo, wo)
        c_e = rot(w_e * v_up, -1, 0)
        c_o = rot(w_o * v_dn, 1, 0)
        p_es = rot(p_e[t], -1, 0)
        p_os = rot(p_o[t], 1, 0)
        terms = []
        for patch, own, side in ((p_e[t], a_e, b_e), (p_o[t], a_o, b_o), (p_es, c_e, None), (p_os, c_o, None)):
            spread = jnp.where(patch > 0, -0.125, 0.0)
            entry = [patch, 0.875 * own, spread * own]
            if side is not None:
                entry += [0.875 * side, spread * side]
            terms.append(entry)
        level.append((terms, w_e * v_e[t], w_o * v_o[t]))
        coarse.append((g_e[t] + g_o[t], v_up, we + wo))
    own_rows = slice(HALO // 2, n1 - HALO // 2)
    for index in (1, 2):
        moved = jnp.where(lane < LANES - HALO, rot(level[0][index], -HALO, 1), rot(level[1][index], -HALO, 1))
        w0_ref[index - 1] = moved[own_rows]

    m_in = selection(2 * LANES, lambda x, j: x // 2 == j)
    m_out = selection(2 * LANES, lambda x, j: x // 2 + 2 * (x % 2) - 1 == j)
    m_even = selection(2 * LANES, lambda x, j: x == 2 * j)
    m_both = jnp.concatenate([m_in, m_out], axis=0)

    def wide(index):
        return jnp.concatenate([coarse[0][index], coarse[1][index]], axis=1)

    zeros = jnp.zeros((c1_ref.shape[1] - n1, LANES), F32)
    c1_ref[0, 0:n1] = dot01(wide(0), m_in)
    c1_ref[1, 0:n1] = dot01(wide(1), m_in)
    c1_ref[2, 0:n1] = dot01(wide(2), m_even)
    for index in range(3):
        c1_ref[index, n1:] = zeros
    for k in range(RHS):
        parts_a = []
        parts_b = []
        for t in range(2):
            terms = level[t][0]
            tests = [entry[0] == k + 1.0 for entry in terms]
            picked = [jnp.where(test, entry[1], entry[2]) for test, entry in zip(tests, terms)]
            parts_a.append((picked[0] + picked[1]) + (picked[2] + picked[3]))
            parts_b.append(
                jnp.where(tests[0], terms[0][3], terms[0][4]) + jnp.where(tests[1], terms[1][3], terms[1][4])
            )
        r1_ref[k, 0:n1] = dot01(jnp.concatenate(parts_a + parts_b, axis=1), m_both)
        r1_ref[k, n1:] = zeros

    k_in = m_in[:LANES]
    k_out = m_out[:LANES]
    k_even = m_even[:LANES]
    k_both = jnp.concatenate([k_in, k_out], axis=0)
    l_in = selection(LANES, lambda x, j: x // 2 - 1 == j % 8)
    l_out = selection(LANES, lambda x, j: x // 2 + 2 * (x % 2) - 2 == j % 8)
    l_even = selection(LANES, lambda x, j: (x // 2 - 1 == j % 8) & (x % 2 == 0))
    l_both = jnp.concatenate([l_in, l_out], axis=0)
    smooth = []
    for r_ref, c_ref, next_r, next_c in (
        (r1_ref, c1_ref, r2_ref, c2_ref),
        (r2_ref, c2_ref, r3_ref, c3_ref),
        (r3_ref, c3_ref, None, None),
    ):
        half = r_ref.shape[1] // 2
        even, uneven = pl.ds(0, half, stride=2), pl.ds(1, half, stride=2)
        odd_lane = iota((half, LANES), 1) % 2 == 1
        ge, go = c_ref[0, even, :], c_ref[0, uneven, :]
        v_up, v_in = c_ref[1, even, :], c_ref[1, uneven, :]
        we, wo = c_ref[2, even, :], c_ref[2, uneven, :]
        ee, eo = rot(we, -1, 1), rot(wo, -1, 1)
        v_dn = rot(v_up, -1, 0)
        w_e = weights_of(ge + v_up + v_in + we + ee)
        w_o = weights_of(go + v_in + v_dn + wo + eo)
        a_e = (1.0 - OMEGA) + w_e * (v_in + jnp.where(odd_lane, we, ee))
        a_o = (1.0 - OMEGA) + w_o * (v_in + jnp.where(odd_lane, wo, eo))
        b_e = w_e * jnp.where(odd_lane, ee, we)
        b_o = w_o * jnp.where(odd_lane, eo, wo)
        c_e = w_e * v_up
        c_o = w_o * v_dn
        smooth.append((w_e, w_o))
        both, inner, evens = (k_both, k_in, k_even) if next_r is not None else (l_both, l_in, l_even)
        coarser = [dot01(ge + go, inner), dot01(v_up, inner), dot01(we + wo, evens)]
        fields = []
        for k in range(RHS):
            re, ro = r_ref[k, even, :], r_ref[k, uneven, :]
            own = a_e * re + a_o * ro + rot(c_o * ro, 1, 0) + rot(c_e * re, -1, 0)
            side = b_e * re + b_o * ro
            fields.append(dot01(jnp.concatenate([own, side], axis=1), both))
        if next_r is not None:
            for index in range(3):
                next_c[index] = coarser[index]
            for k in range(RHS):
                next_r[k] = fields[k]

    shape = fields[0].shape
    mine = iota(shape, 1) // 8 == iota(shape, 0) - 1

    def flat(field):
        return jnp.sum(jnp.where(mine, field, 0.0), axis=0, keepdims=True)

    sub = iota((8, LANES), 0)
    lane8 = iota((8, LANES), 1)
    links = jnp.where(sub < 4, flat(coarser[1]), flat(coarser[2]))
    turned = rot(links, 96, 1)
    for row in (1, 2):
        turned = jnp.where(sub % 4 == row, rot(links, 96 - 32 * row, 1), turned)
    tile = jnp.broadcast_to(flat(coarser[0]), (8, LANES))
    for k in range(RHS - 1):
        tile = jnp.where(sub == k, flat(fields[k]), tile)
    tile = jnp.where(lane8 < 96, tile, turned)

    @pl.loop(0, devices)
    def _(device):
        payload_ref[device] = tile

    spread = selection(LANES, lambda j, x: x // 2 == j)
    for k in range(RHS):
        w_e, w_o = smooth[2]
        half = w_e.shape[0]
        t3_ref[k, pl.ds(0, half, stride=2), :] = w_e * r3_ref[k, pl.ds(0, half, stride=2), :]
        t3_ref[k, pl.ds(1, half, stride=2), :] = w_o * r3_ref[k, pl.ds(1, half, stride=2), :]
    for k in range(RHS):
        w_e, w_o = smooth[1]
        half = w_e.shape[0]
        finer = dot01(t3_ref[k], spread)
        t2_ref[k, pl.ds(0, half, stride=2), :] = finer + w_e * r2_ref[k, pl.ds(0, half, stride=2), :]
        t2_ref[k, pl.ds(1, half, stride=2), :] = finer + w_o * r2_ref[k, pl.ds(1, half, stride=2), :]
    for k in range(RHS):
        w_e, w_o = smooth[0]
        half = w_e.shape[0]
        finer = dot01(t2_ref[k], spread)
        t1_ref[k, pl.ds(0, half, stride=2), :] = finer + w_e * r1_ref[k, pl.ds(0, half, stride=2), :]
        t1_ref[k, pl.ds(1, half, stride=2), :] = finer + w_o * r1_ref[k, pl.ds(1, half, stride=2), :]


def solve_kernel(grid, me_ref, all_ref, t1_ref, w0_ref, patch_ref, out_ref, coef_ref, x_ref, r_ref, p_ref, q_ref, u_ref):
    grid_rows, grid_cols = grid
    count = grid_rows * grid_cols
    lane = iota((8, LANES), 1)
    sub = iota((8, LANES), 0)
    inside = lane < 96

    def choose(test, yes, no):
        if isinstance(test, bool):
            return yes if test else no
        return jnp.where(test, yes, no)

    def every(body, init):
        if count <= 64:
            for tile in range(count):
                init = body(tile, init)
            return init
        return lax.fori_loop(0, count, body, init)

    def above(ref, t):
        return jnp.where(lane < 8, rot(ref[choose(t >= grid_cols, t - grid_cols, t)], 40, 1), rot(ref[t], 8, 1))

    def below(ref, t):
        near = ref[choose(t + grid_cols < count, t + grid_cols, t)]
        return jnp.where(lane >= 88, rot(near, 88, 1), rot(ref[t], 120, 1))

    def left(ref, t):
        near = ref[choose(t % grid_cols > 0, t - 1, t)]
        return jnp.where(lane % 8 == 0, rot(near, 121, 1), rot(ref[t], 1, 1))

    def right(ref, t):
        near = ref[choose(t % grid_cols < grid_cols - 1, t + 1, t)]
        return jnp.where(lane % 8 == 7, rot(near, 7, 1), rot(ref[t], 127, 1))

    def unpack(t, rr):
        tile = all_ref[t]
        known = jnp.where(inside & (sub < 7), tile, 0.0)
        rhs = jnp.where(sub < 7, known, -jnp.sum(known, axis=0, keepdims=True))
        r_ref[t] = rhs
        p_ref[t] = rhs
        coef_ref[0, t] = jnp.where(inside, jnp.broadcast_to(tile[7:8], (8, LANES)), 0.0)
        turned = jnp.zeros((8, LANES), F32)
        for row in range(3):
            turned = jnp.where((sub % 4 == row) & (lane // 32 == row), rot(tile, 32 * row + 32, 1), turned)
        north = jnp.sum(jnp.where(sub < 4, turned, 0.0), axis=0, keepdims=True)
        west = jnp.sum(jnp.where(sub < 4, 0.0, turned), axis=0, keepdims=True)
        coef_ref[1, t] = jnp.broadcast_to(north, (8, LANES))
        coef_ref[3, t] = jnp.broadcast_to(west, (8, LANES))
        return rr + rhs * rhs

    def total(values):
        return jnp.sum(values, axis=1, keepdims=True)

    zero = jnp.zeros((8, LANES), F32)
    rr = total(every(unpack, zero))

    def finish(t, carry):
        south = below(coef_ref.at[1], t)
        bottom = choose(t + grid_cols < count, 1.0, 0.0)
        south = jnp.where(lane < 88, south, jnp.where(inside, south * bottom, 0.0))
        east = right(coef_ref.at[3], t)
        last = choose(t % grid_cols < grid_cols - 1, 1.0, 0.0)
        east = jnp.where(inside, jnp.where(lane % 8 == 7, east * last, east), 0.0)
        coef_ref[2, t] = south
        coef_ref[4, t] = east
        coef_ref[0, t] = coef_ref[0, t] + coef_ref[1, t] + south + coef_ref[3, t] + east
        return carry

    every(finish, 0)

    def image_of(t, dot):
        here = p_ref[t]
        pulled = coef_ref[1, t] * above(p_ref, t) + coef_ref[2, t] * below(p_ref, t)
        pulled = pulled + coef_ref[3, t] * left(p_ref, t) + coef_ref[4, t] * right(p_ref, t)
        image = coef_ref[0, t] * here - pulled
        q_ref[t] = image
        return dot + here * image

    for sweep in range(ITERS):
        step = jnp.broadcast_to(rr / total(every(image_of, zero)), (8, LANES))

        def advance(t, norm):
            gain = step * p_ref[t]
            x_ref[t] = gain if sweep == 0 else x_ref[t] + gain
            if sweep + 1 == ITERS:
                return norm
            left_over = r_ref[t] - step * q_ref[t]
            r_ref[t] = left_over
            return norm + left_over * left_over

        norm = every(advance, zero)
        if sweep + 1 < ITERS:
            new = total(norm)
            ratio = jnp.broadcast_to(new / rr, (8, LANES))
            rr = new

            def turn(t, carry):
                p_ref[t] = r_ref[t] + ratio * p_ref[t]
                return carry

            every(turn, 0)

    mine = x_ref[me_ref[0]]
    groups = u_ref.shape[0] // 8
    stacked = jnp.concatenate([jnp.where(lane // 8 == i, mine, 0.0) for i in range(groups)], axis=0)
    widen = selection(LANES, lambda x, j: (j >= 8) & (j < 72) & (x % 8 == (j - 8) // 8))
    u_ref[...] = dot01(stacked, widen)
    spread = selection(LANES, lambda j, x: j == x // 2 + 8)
    half = w0_ref.shape[1]
    even, uneven = pl.ds(0, half, stride=2), pl.ds(1, half, stride=2)
    sides = []
    for index, rows in ((0, even), (1, uneven)):
        weight = w0_ref[index]
        patch = patch_ref[rows, :]
        sides.append((rows, patch, 0.875 * weight, jnp.where(patch > 0, -0.125, 0.0) * weight))
    for k in range(RHS):
        coarse = jnp.concatenate(
            [t1_ref[k, pl.ds(8 * i + 8, 8), :] + u_ref[pl.ds(8 * i + k, 1), :] for i in range(groups)], axis=0
        )
        finer = dot01(coarse, spread)
        for rows, patch, chosen, other in sides:
            out_ref[k, rows, :] = finer + jnp.where(patch == k + 1, chosen, other)


def shifted(block, axis, distance):
    devices = range(lax.axis_size(axis))
    return lax.ppermute(block, axis, [(i, i + distance) for i in devices if i + distance in devices])


def shards(resistance, ground, nodata, patch_ids):
    grid = (lax.axis_size("row"), lax.axis_size("col"))
    devices = grid[0] * grid[1]
    rows, cols = resistance.shape
    own = (resistance, ground, nodata, patch_ids)
    shape = jax.ShapeDtypeStruct
    strip = shape((4 * HALO, cols), F32)
    down, up = pl.pallas_call(pack_rows_kernel, out_shape=(strip, strip), name="pack_rows")(*own)
    above = shifted(down, "row", 1)
    below = shifted(up, "row", -1)
    tall = rows + 2 * HALO
    strip = shape((tall // 2, LANES), F32)
    to_right, to_left = pl.pallas_call(pack_cols_kernel, out_shape=(strip, strip), name="pack_cols")(
        *own, above, below
    )
    left = shifted(to_right, "col", 1)
    right = shifted(to_left, "col", -1)
    sizes = [128, 64, 32]
    payload, t1, w0 = pl.pallas_call(
        down_kernel,
        out_shape=(
            shape((devices, 8, LANES), F32),
            shape((RHS, sizes[0], LANES), F32),
            shape((2, rows // 2, LANES), F32),
        ),
        scratch_shapes=[pltpu.VMEM((8, tall, LANES), F32)]
        + [pltpu.VMEM((RHS, size, LANES), F32) for size in sizes]
        + [pltpu.VMEM((3, size, LANES), F32) for size in sizes]
        + [pltpu.VMEM((RHS, size, LANES), F32) for size in sizes[:0:-1]],
        name="down",
    )(*own, above, below, left, right)
    everything = lax.all_to_all(payload, ("row", "col"), 0, 0)
    me = (lax.axis_index("row") * grid[1] + lax.axis_index("col")).reshape(1).astype(jnp.int32)
    field = pltpu.VMEM((devices, 8, LANES), F32)
    vmem = pl.BlockSpec(memory_space=pltpu.VMEM)
    return pl.pallas_call(
        functools.partial(solve_kernel, grid),
        out_shape=shape((RHS, rows, cols), F32),
        in_specs=[pl.BlockSpec(memory_space=pltpu.SMEM)] + [vmem] * 4,
        scratch_shapes=[pltpu.VMEM((5, devices, 8, LANES), F32)]
        + [field] * 4
        + [pltpu.VMEM((rows // 16 * 8, LANES), F32)],
        name="solve",
    )(me, everything, t1, w0, patch_ids)


def solution(mesh):
    spec = P("row", "col")
    return jax.shard_map(shards, mesh=mesh, in_specs=(spec,) * 4, out_specs=P(None, "row", "col"), check_vma=False)
```

```python
import functools

import jax
import jax.numpy as jnp
from jax import lax
from jax.experimental import pallas as pl
from jax.experimental.pallas import tpu as pltpu
from jax.sharding import PartitionSpec as P

RHS = 8
ITERS = 4
OMEGA = 0.8
HALO = 16
LANES = 128
F32 = jnp.float32
BF16 = jnp.bfloat16
PIECES = 3


def iota(shape, dim):
    return lax.broadcasted_iota(jnp.int32, shape, dim)


def selection(rows, test):
    shape = (rows, LANES)
    return jnp.where(test(iota(shape, 0), iota(shape, 1)), 1.0, 0.0).astype(BF16)


def dot01(values, matrix, pieces=PIECES):
    total = None
    for piece in range(pieces):
        part = values.astype(BF16)
        term = jnp.dot(part, matrix, preferred_element_type=F32)
        total = term if total is None else total + term
        if piece + 1 < pieces:
            values = values - part.astype(F32)
    return total


def rot(values, shift, axis):
    return pltpu.roll(values, shift % values.shape[axis], axis)


def lanes_of(values, lane):
    return iota(values.shape, 1) if lane is None else lane


def pack_rows_kernel(res_ref, ground_ref, nodata_ref, patch_ref, own_ref, down_ref, up_ref):
    rows = res_ref.shape[0]
    fields = (
        res_ref[...],
        ground_ref[...],
        jnp.where(nodata_ref[...] == 0, 1.0, 0.0),
        patch_ref[...].astype(F32),
    )
    for which, values in enumerate(fields):
        own_ref[which] = values
        down_ref[pl.ds(which * HALO, HALO)] = values[rows - HALO :]
        up_ref[pl.ds(which * HALO, HALO)] = values[:HALO]


def pack_cols_kernel(own_ref, above_ref, below_ref, tall_ref, right_ref, left_ref):
    half = own_ref.shape[1] // 2
    tall = []
    for which in range(4):
        part = pl.ds(which * HALO, HALO)
        upper = jnp.concatenate([above_ref[part], own_ref[which, :half]], axis=0)
        lower = jnp.concatenate([own_ref[which, half:], below_ref[part]], axis=0)
        tall_ref[which, : half + HALO] = upper
        tall_ref[which, half + HALO :] = lower
        tall.append((upper, lower))
    shape = right_ref.shape
    group_of = iota(shape, 1) // HALO
    to_right = jnp.zeros(shape, F32)
    to_left = jnp.zeros(shape, F32)
    for which in range(4):
        for side in range(2):
            group = 2 * which + side
            values = tall[which][side]
            here = group_of == group
            to_right = jnp.where(here, rot(values, HALO * group + HALO, 1), to_right)
            to_left = jnp.where(here, rot(values, HALO * group, 1), to_left)
    right_ref[...] = to_right
    left_ref[...] = to_left


def link(resist, validity, near_resist, near_valid):
    return (validity * near_valid) * (2.0 / (resist + near_resist))


def weights_of(diag):
    return OMEGA / jnp.where(diag > 0, diag, 1.0)


def down_kernel(
    tall_ref,
    left_ref,
    right_ref,
    payload_ref,
    t1_ref,
    w0_ref,
    ext_ref,
    r1_ref,
    r2_ref,
    r3_ref,
    c1_ref,
    c2_ref,
    c3_ref,
    t3_ref,
    t2_ref,
):
    devices = payload_ref.shape[0]
    quarter = tall_ref.shape[1] // 2
    lane = iota((quarter, LANES), 1)
    from_left = left_ref[...]
    from_right = right_ref[...]
    for which in range(4):
        for side in range(2):
            group = 2 * which + side
            moved = rot(tall_ref[which, pl.ds(side * quarter, quarter)], HALO, 1)
            tile0 = jnp.where(lane < HALO, rot(from_left, -HALO * group, 1), moved)
            tile1 = jnp.where(
                lane < HALO,
                moved,
                jnp.where(lane < 2 * HALO, rot(from_right, HALO - HALO * group, 1), 0.0),
            )
            if which < 2:
                tile0 = jnp.where(tile0 > 0, tile0, 1.0)
                tile1 = jnp.where(tile1 > 0, tile1, 1.0)
            ext_ref[2 * which, pl.ds(side * quarter, quarter), :] = tile0
            ext_ref[2 * which + 1, pl.ds(side * quarter, quarter), :] = tile1

    n1 = quarter
    odd = lane % 2 == 1

    def parity(which, start):
        return [ext_ref[2 * which + tile, pl.ds(start, n1, stride=2), :] for tile in range(2)]

    res_e, res_o = parity(0, 0), parity(0, 1)
    g_e, g_o = parity(1, 0), parity(1, 1)
    v_e, v_o = parity(2, 0), parity(2, 1)
    p_e, p_o = parity(3, 0), parity(3, 1)

    def left_of(pair):
        first, second = rot(pair[0], 1, 1), rot(pair[1], 1, 1)
        return [first, jnp.where(lane == 0, first, second)]

    def right_of(pair):
        first, second = rot(pair[0], -1, 1), rot(pair[1], -1, 1)
        return [jnp.where(lane == LANES - 1, second, first), second]

    west = {}
    for name, res, val in (("e", res_e, v_e), ("o", res_o, v_o)):
        near_res, near_val = left_of(res), left_of(val)
        west[name] = [link(res[t], val[t], near_res[t], near_val[t]) for t in range(2)]
    east = {name: right_of(pair) for name, pair in west.items()}
    level = []
    coarse = []
    for t in range(2):
        v_in = link(res_e[t], v_e[t], res_o[t], v_o[t])
        v_up = link(res_e[t], v_e[t], rot(res_o[t], 1, 0), rot(v_o[t], 1, 0))
        v_dn = rot(v_up, -1, 0)
        we, wo, ee, eo = west["e"][t], west["o"][t], east["e"][t], east["o"][t]
        w_e = weights_of(g_e[t] + v_up + v_in + we + ee)
        w_o = weights_of(g_o[t] + v_in + v_dn + wo + eo)
        a_e = (1.0 - OMEGA) * v_e[t] + w_e * (v_in + jnp.where(odd, we, ee))
        a_o = (1.0 - OMEGA) * v_o[t] + w_o * (v_in + jnp.where(odd, wo, eo))
        b_e = w_e * jnp.where(odd, ee, we)
        b_o = w_o * jnp.where(odd, eo, wo)
        c_e = rot(w_e * v_up, -1, 0)
        c_o = rot(w_o * v_dn, 1, 0)
        p_es = rot(p_e[t], -1, 0)
        p_os = rot(p_o[t], 1, 0)
        terms = []
        for patch, own, side in ((p_e[t], a_e, b_e), (p_o[t], a_o, b_o), (p_es, c_e, None), (p_os, c_o, None)):
            spread = jnp.where(patch > 0, -0.125, 0.0)
            entry = [patch, 0.875 * own, spread * own]
            if side is not None:
                entry += [0.875 * side, spread * side]
            terms.append(entry)
        level.append((terms, w_e * v_e[t], w_o * v_o[t]))
        coarse.append((g_e[t] + g_o[t], v_up, we + wo))
    own_rows = slice(HALO // 2, n1 - HALO // 2)
    for index in (1, 2):
        moved = jnp.where(lane < LANES - HALO, rot(level[0][index], -HALO, 1), rot(level[1][index], -HALO, 1))
        w0_ref[index - 1] = moved[own_rows]

    m_in = selection(2 * LANES, lambda x, j: x // 2 == j)
    m_out = selection(2 * LANES, lambda x, j: x // 2 + 2 * (x % 2) - 1 == j)
    m_even = selection(2 * LANES, lambda x, j: x == 2 * j)
    m_both = jnp.concatenate([m_in, m_out], axis=0)

    def wide(index):
        return jnp.concatenate([coarse[0][index], coarse[1][index]], axis=1)

    zeros = jnp.zeros((c1_ref.shape[1] - n1, LANES), F32)
    c1_ref[0, 0:n1] = dot01(wide(0), m_in)
    c1_ref[1, 0:n1] = dot01(wide(1), m_in)
    c1_ref[2, 0:n1] = dot01(wide(2), m_even)
    for index in range(3):
        c1_ref[index, n1:] = zeros
    for k in range(RHS):
        parts_a = []
        parts_b = []
        for t in range(2):
            terms = level[t][0]
            tests = [entry[0] == k + 1.0 for entry in terms]
            picked = [jnp.where(test, entry[1], entry[2]) for test, entry in zip(tests, terms)]
            parts_a.append((picked[0] + picked[1]) + (picked[2] + picked[3]))
            parts_b.append(
                jnp.where(tests[0], terms[0][3], terms[0][4]) + jnp.where(tests[1], terms[1][3], terms[1][4])
            )
        r1_ref[k, 0:n1] = dot01(jnp.concatenate(parts_a + parts_b, axis=1), m_both)
        r1_ref[k, n1:] = zeros

    k_in = m_in[:LANES]
    k_out = m_out[:LANES]
    k_even = m_even[:LANES]
    k_both = jnp.concatenate([k_in, k_out], axis=0)
    l_in = selection(LANES, lambda x, j: x // 2 - 1 == j % 8)
    l_out = selection(LANES, lambda x, j: x // 2 + 2 * (x % 2) - 2 == j % 8)
    l_even = selection(LANES, lambda x, j: (x // 2 - 1 == j % 8) & (x % 2 == 0))
    l_both = jnp.concatenate([l_in, l_out], axis=0)
    smooth = []
    for r_ref, c_ref, next_r, next_c in (
        (r1_ref, c1_ref, r2_ref, c2_ref),
        (r2_ref, c2_ref, r3_ref, c3_ref),
        (r3_ref, c3_ref, None, None),
    ):
        half = r_ref.shape[1] // 2
        even, uneven = pl.ds(0, half, stride=2), pl.ds(1, half, stride=2)
        odd_lane = iota((half, LANES), 1) % 2 == 1
        ge, go = c_ref[0, even, :], c_ref[0, uneven, :]
        v_up, v_in = c_ref[1, even, :], c_ref[1, uneven, :]
        we, wo = c_ref[2, even, :], c_ref[2, uneven, :]
        ee, eo = rot(we, -1, 1), rot(wo, -1, 1)
        v_dn = rot(v_up, -1, 0)
        w_e = weights_of(ge + v_up + v_in + we + ee)
        w_o = weights_of(go + v_in + v_dn + wo + eo)
        a_e = (1.0 - OMEGA) + w_e * (v_in + jnp.where(odd_lane, we, ee))
        a_o = (1.0 - OMEGA) + w_o * (v_in + jnp.where(odd_lane, wo, eo))
        b_e = w_e * jnp.where(odd_lane, ee, we)
        b_o = w_o * jnp.where(odd_lane, eo, wo)
        c_e = w_e * v_up
        c_o = w_o * v_dn
        smooth.append((w_e, w_o))
        both, inner, evens = (k_both, k_in, k_even) if next_r is not None else (l_both, l_in, l_even)
        coarser = [dot01(ge + go, inner), dot01(v_up, inner), dot01(we + wo, evens)]
        fields = []
        for k in range(RHS):
            re, ro = r_ref[k, even, :], r_ref[k, uneven, :]
            own = a_e * re + a_o * ro + rot(c_o * ro, 1, 0) + rot(c_e * re, -1, 0)
            side = b_e * re + b_o * ro
            fields.append(dot01(jnp.concatenate([own, side], axis=1), both))
        if next_r is not None:
            for index in range(3):
                next_c[index] = coarser[index]
            for k in range(RHS):
                next_r[k] = fields[k]

    shape = fields[0].shape
    mine = iota(shape, 1) // 8 == iota(shape, 0) - 1

    def flat(field):
        return jnp.sum(jnp.where(mine, field, 0.0), axis=0, keepdims=True)

    sub = iota((8, LANES), 0)
    lane8 = iota((8, LANES), 1)
    links = jnp.where(sub < 4, flat(coarser[1]), flat(coarser[2]))
    turned = rot(links, 96, 1)
    for row in (1, 2):
        turned = jnp.where(sub % 4 == row, rot(links, 96 - 32 * row, 1), turned)
    tile = jnp.broadcast_to(flat(coarser[0]), (8, LANES))
    for k in range(RHS - 1):
        tile = jnp.where(sub == k, flat(fields[k]), tile)
    tile = jnp.where(lane8 < 96, tile, turned)

    @pl.loop(0, devices)
    def _(device):
        payload_ref[device] = tile

    spread = selection(LANES, lambda j, x: x // 2 == j)
    for k in range(RHS):
        w_e, w_o = smooth[2]
        half = w_e.shape[0]
        t3_ref[k, pl.ds(0, half, stride=2), :] = w_e * r3_ref[k, pl.ds(0, half, stride=2), :]
        t3_ref[k, pl.ds(1, half, stride=2), :] = w_o * r3_ref[k, pl.ds(1, half, stride=2), :]
    for k in range(RHS):
        w_e, w_o = smooth[1]
        half = w_e.shape[0]
        finer = dot01(t3_ref[k], spread)
        t2_ref[k, pl.ds(0, half, stride=2), :] = finer + w_e * r2_ref[k, pl.ds(0, half, stride=2), :]
        t2_ref[k, pl.ds(1, half, stride=2), :] = finer + w_o * r2_ref[k, pl.ds(1, half, stride=2), :]
    for k in range(RHS):
        w_e, w_o = smooth[0]
        half = w_e.shape[0]
        finer = dot01(t2_ref[k], spread)
        t1_ref[k, pl.ds(0, half, stride=2), :] = finer + w_e * r1_ref[k, pl.ds(0, half, stride=2), :]
        t1_ref[k, pl.ds(1, half, stride=2), :] = finer + w_o * r1_ref[k, pl.ds(1, half, stride=2), :]


def solve_kernel(grid, me_ref, all_ref, t1_ref, w0_ref, patch_ref, out_ref, coef_ref, x_ref, r_ref, p_ref, q_ref, u_ref):
    grid_rows, grid_cols = grid
    count = grid_rows * grid_cols
    lane = iota((8, LANES), 1)
    sub = iota((8, LANES), 0)
    inside = lane < 96

    def choose(test, yes, no):
        if isinstance(test, bool):
            return yes if test else no
        return jnp.where(test, yes, no)

    def every(body, init):
        if count <= 64:
            for tile in range(count):
                init = body(tile, init)
            return init
        return lax.fori_loop(0, count, body, init)

    def above(ref, t):
        return jnp.where(lane < 8, rot(ref[choose(t >= grid_cols, t - grid_cols, t)], 40, 1), rot(ref[t], 8, 1))

    def below(ref, t):
        near = ref[choose(t + grid_cols < count, t + grid_cols, t)]
        return jnp.where(lane >= 88, rot(near, 88, 1), rot(ref[t], 120, 1))

    def left(ref, t):
        near = ref[choose(t % grid_cols > 0, t - 1, t)]
        return jnp.where(lane % 8 == 0, rot(near, 121, 1), rot(ref[t], 1, 1))

    def right(ref, t):
        near = ref[choose(t % grid_cols < grid_cols - 1, t + 1, t)]
        return jnp.where(lane % 8 == 7, rot(near, 7, 1), rot(ref[t], 127, 1))

    def unpack(t, rr):
        tile = all_ref[t]
        known = jnp.where(inside & (sub < 7), tile, 0.0)
        rhs = jnp.where(sub < 7, known, -jnp.sum(known, axis=0, keepdims=True))
        r_ref[t] = rhs
        p_ref[t] = rhs
        coef_ref[0, t] = jnp.where(inside, jnp.broadcast_to(tile[7:8], (8, LANES)), 0.0)
        turned = jnp.zeros((8, LANES), F32)
        for row in range(3):
            turned = jnp.where((sub % 4 == row) & (lane // 32 == row), rot(tile, 32 * row + 32, 1), turned)
        north = jnp.sum(jnp.where(sub < 4, turned, 0.0), axis=0, keepdims=True)
        west = jnp.sum(jnp.where(sub < 4, 0.0, turned), axis=0, keepdims=True)
        coef_ref[1, t] = jnp.broadcast_to(north, (8, LANES))
        coef_ref[3, t] = jnp.broadcast_to(west, (8, LANES))
        return rr + rhs * rhs

    def total(values):
        return jnp.sum(values, axis=1, keepdims=True)

    zero = jnp.zeros((8, LANES), F32)
    rr = total(every(unpack, zero))

    def finish(t, carry):
        south = below(coef_ref.at[1], t)
        bottom = choose(t + grid_cols < count, 1.0, 0.0)
        south = jnp.where(lane < 88, south, jnp.where(inside, south * bottom, 0.0))
        east = right(coef_ref.at[3], t)
        last = choose(t % grid_cols < grid_cols - 1, 1.0, 0.0)
        east = jnp.where(inside, jnp.where(lane % 8 == 7, east * last, east), 0.0)
        coef_ref[2, t] = south
        coef_ref[4, t] = east
        coef_ref[0, t] = coef_ref[0, t] + coef_ref[1, t] + south + coef_ref[3, t] + east
        return carry

    every(finish, 0)

    def image_of(t, dot):
        here = p_ref[t]
        pulled = coef_ref[1, t] * above(p_ref, t) + coef_ref[2, t] * below(p_ref, t)
        pulled = pulled + coef_ref[3, t] * left(p_ref, t) + coef_ref[4, t] * right(p_ref, t)
        image = coef_ref[0, t] * here - pulled
        q_ref[t] = image
        return dot + here * image

    for sweep in range(ITERS):
        step = jnp.broadcast_to(rr / total(every(image_of, zero)), (8, LANES))

        def advance(t, norm):
            gain = step * p_ref[t]
            x_ref[t] = gain if sweep == 0 else x_ref[t] + gain
            if sweep + 1 == ITERS:
                return norm
            left_over = r_ref[t] - step * q_ref[t]
            r_ref[t] = left_over
            return norm + left_over * left_over

        norm = every(advance, zero)
        if sweep + 1 < ITERS:
            new = total(norm)
            ratio = jnp.broadcast_to(new / rr, (8, LANES))
            rr = new

            def turn(t, carry):
                p_ref[t] = r_ref[t] + ratio * p_ref[t]
                return carry

            every(turn, 0)

    mine = x_ref[me_ref[0]]
    groups = u_ref.shape[0] // 8
    stacked = jnp.concatenate([jnp.where(lane // 8 == i, mine, 0.0) for i in range(groups)], axis=0)
    widen = selection(LANES, lambda x, j: (j >= 8) & (j < 72) & (x % 8 == (j - 8) // 8))
    u_ref[...] = dot01(stacked, widen)
    spread = selection(LANES, lambda j, x: j == x // 2 + 8)
    half = w0_ref.shape[1]
    even, uneven = pl.ds(0, half, stride=2), pl.ds(1, half, stride=2)
    sides = []
    for index, rows in ((0, even), (1, uneven)):
        weight = w0_ref[index]
        patch = patch_ref[rows, :]
        sides.append((rows, patch, 0.875 * weight, jnp.where(patch > 0, -0.125, 0.0) * weight))
    for k in range(RHS):
        coarse = jnp.concatenate(
            [t1_ref[k, pl.ds(8 * i + 8, 8), :] + u_ref[pl.ds(8 * i + k, 1), :] for i in range(groups)], axis=0
        )
        finer = dot01(coarse, spread)
        for rows, patch, chosen, other in sides:
            out_ref[k, rows, :] = finer + jnp.where(patch == k + 1, chosen, other)


def shifted(block, axis, distance):
    devices = range(lax.axis_size(axis))
    return lax.ppermute(block, axis, [(i, i + distance) for i in devices if i + distance in devices])


def shards(resistance, ground, nodata, patch_ids):
    grid = (lax.axis_size("row"), lax.axis_size("col"))
    devices = grid[0] * grid[1]
    rows, cols = resistance.shape
    own = (resistance, ground, nodata, patch_ids)
    shape = jax.ShapeDtypeStruct
    vmem = pl.BlockSpec(memory_space=pltpu.VMEM)

    def near(value):
        return pltpu.with_memory_space_constraint(value, pltpu.VMEM)

    strip = pltpu.VMEM((4 * HALO, cols), F32)
    kept, down, up = pl.pallas_call(
        pack_rows_kernel, out_shape=(pltpu.VMEM((4, rows, cols), F32), strip, strip), name="pack_rows"
    )(*own)
    above = near(shifted(down, "row", 1))
    below = near(shifted(up, "row", -1))
    tall_rows = rows + 2 * HALO
    strip = pltpu.VMEM((tall_rows // 2, LANES), F32)
    tall, to_right, to_left = pl.pallas_call(
        pack_cols_kernel, out_shape=(pltpu.VMEM((4, tall_rows, cols), F32), strip, strip), name="pack_cols"
    )(near(kept), above, below)
    left = near(shifted(to_right, "col", 1))
    right = near(shifted(to_left, "col", -1))
    sizes = [128, 64, 32]
    payload, t1, w0 = pl.pallas_call(
        down_kernel,
        out_shape=(
            pltpu.VMEM((devices, 8, LANES), F32),
            pltpu.VMEM((RHS, sizes[0], LANES), F32),
            pltpu.VMEM((2, rows // 2, LANES), F32),
        ),
        scratch_shapes=[pltpu.VMEM((8, tall_rows, LANES), F32)]
        + [pltpu.VMEM((RHS, size, LANES), F32) for size in sizes]
        + [pltpu.VMEM((3, size, LANES), F32) for size in sizes]
        + [pltpu.VMEM((RHS, size, LANES), F32) for size in sizes[:0:-1]],
        name="down",
    )(near(tall), left, right)
    everything = near(lax.all_to_all(payload, ("row", "col"), 0, 0))
    me = (lax.axis_index("row") * grid[1] + lax.axis_index("col")).reshape(1).astype(jnp.int32)
    field = pltpu.VMEM((devices, 8, LANES), F32)
    return pl.pallas_call(
        functools.partial(solve_kernel, grid),
        out_shape=shape((RHS, rows, cols), F32),
        in_specs=[pl.BlockSpec(memory_space=pltpu.SMEM)] + [vmem] * 4,
        scratch_shapes=[pltpu.VMEM((5, devices, 8, LANES), F32)]
        + [field] * 4
        + [pltpu.VMEM((rows // 16 * 8, LANES), F32)],
        name="solve",
    )(me, everything, near(t1), near(w0), patch_ids)


def solution(mesh):
    spec = P("row", "col")
    return jax.shard_map(shards, mesh=mesh, in_specs=(spec,) * 4, out_specs=P(None, "row", "col"), check_vma=False)
```

```python
import functools

import jax
import jax.numpy as jnp
from jax import lax
from jax.experimental import pallas as pl
from jax.experimental.pallas import tpu as pltpu
from jax.sharding import PartitionSpec as P

RHS = 8
ITERS = 4
OMEGA = 0.8
HALO = 16
LANES = 128
F32 = jnp.float32
BF16 = jnp.bfloat16
PIECES = 2
VMEM_LIMIT = 32 * 2**20


def iota(shape, dim):
    return lax.broadcasted_iota(jnp.int32, shape, dim)


def selection(rows, test):
    shape = (rows, LANES)
    return jnp.where(test(iota(shape, 0), iota(shape, 1)), 1.0, 0.0).astype(BF16)


def dot01(values, matrix, pieces=PIECES):
    total = None
    for piece in range(pieces):
        part = values.astype(BF16)
        term = jnp.dot(part, matrix, preferred_element_type=F32)
        total = term if total is None else total + term
        if piece + 1 < pieces:
            values = values - part.astype(F32)
    return total


def rot(values, shift, axis):
    return pltpu.roll(values, shift % values.shape[axis], axis)


def lanes_of(values, lane):
    return iota(values.shape, 1) if lane is None else lane


def pack_rows_kernel(
    res_ref, ground_ref, nodata_ref, patch_ref, own_ref, first_ref, second_ref, nodata_near_ref, patch_near_ref, sem_ref
):
    rows = res_ref.shape[0]
    copies = [
        pltpu.make_async_copy(source, target, sem_ref.at[which])
        for which, (source, target) in enumerate(
            (
                (res_ref, own_ref.at[0]),
                (ground_ref, own_ref.at[1]),
                (nodata_ref, nodata_near_ref),
                (patch_ref, patch_near_ref),
            )
        )
    ]
    for copy in copies:
        copy.start()
    for copy in copies:
        copy.wait()
    own_ref[2] = jnp.where(nodata_near_ref[...] == 0, 1.0, 0.0)
    own_ref[3] = patch_near_ref[...].astype(F32)
    odd = lax.axis_index("row") % 2 == 1
    for which in range(4):
        top = own_ref[which, :HALO]
        bottom = own_ref[which, rows - HALO :]
        part = pl.ds(which * HALO, HALO)
        first_ref[part] = jnp.where(odd, top, bottom)
        second_ref[part] = jnp.where(odd, bottom, top)


def before_after(axis, first, second):
    index = lax.axis_index(axis)
    odd = index % 2 == 1
    before = jnp.where(index > 0, jnp.where(odd, first, second), 0.0)
    after = jnp.where(index < lax.axis_size(axis) - 1, jnp.where(odd, second, first), 0.0)
    return before, after


def pack_cols_kernel(own_ref, from_first_ref, from_second_ref, tall_ref, first_ref, second_ref):
    half = own_ref.shape[1] // 2
    shape = first_ref.shape
    group_of = iota(shape, 1) // HALO
    odd = lax.axis_index("col") % 2 == 1
    above, below = before_after("row", from_first_ref[...], from_second_ref[...])
    to_right = jnp.zeros(shape, F32)
    to_left = jnp.zeros(shape, F32)
    for which in range(4):
        part = slice(which * HALO, which * HALO + HALO)
        upper = jnp.concatenate([above[part], own_ref[which, :half]], axis=0)
        lower = jnp.concatenate([own_ref[which, half:], below[part]], axis=0)
        tall_ref[which, : half + HALO] = upper
        tall_ref[which, half + HALO :] = lower
        for side, values in enumerate((upper, lower)):
            group = 2 * which + side
            here = group_of == group
            to_right = jnp.where(here, rot(values, HALO * group + HALO, 1), to_right)
            to_left = jnp.where(here, rot(values, HALO * group, 1), to_left)
    first_ref[...] = jnp.where(odd, to_left, to_right)
    second_ref[...] = jnp.where(odd, to_right, to_left)


def link(resist, validity, near_resist, near_valid):
    return (validity * near_valid) * (2.0 / (resist + near_resist))


def weights_of(diag):
    return OMEGA / jnp.where(diag > 0, diag, 1.0)


def down_kernel(
    tall_ref,
    from_first_ref,
    from_second_ref,
    payload_ref,
    w0_ref,
    r1_ref,
    r2_ref,
    r3_ref,
    w1_ref,
    w2_ref,
    w3_ref,
    ext_ref,
    c1_ref,
    c2_ref,
    c3_ref,
):
    devices = payload_ref.shape[0]
    quarter = tall_ref.shape[1] // 2
    lane = iota((quarter, LANES), 1)
    from_left, from_right = before_after("col", from_first_ref[...], from_second_ref[...])
    for which in range(4):
        for side in range(2):
            group = 2 * which + side
            moved = rot(tall_ref[which, pl.ds(side * quarter, quarter)], HALO, 1)
            tile0 = jnp.where(lane < HALO, rot(from_left, -HALO * group, 1), moved)
            tile1 = jnp.where(
                lane < HALO,
                moved,
                jnp.where(lane < 2 * HALO, rot(from_right, HALO - HALO * group, 1), 0.0),
            )
            if which < 2:
                tile0 = jnp.where(tile0 > 0, tile0, 1.0)
                tile1 = jnp.where(tile1 > 0, tile1, 1.0)
            ext_ref[2 * which, pl.ds(side * quarter, quarter), :] = tile0
            ext_ref[2 * which + 1, pl.ds(side * quarter, quarter), :] = tile1

    n1 = quarter
    odd = lane % 2 == 1

    def parity(which, start):
        return [ext_ref[2 * which + tile, pl.ds(start, n1, stride=2), :] for tile in range(2)]

    res_e, res_o = parity(0, 0), parity(0, 1)
    g_e, g_o = parity(1, 0), parity(1, 1)
    v_e, v_o = parity(2, 0), parity(2, 1)
    p_e, p_o = parity(3, 0), parity(3, 1)

    def left_of(pair):
        first, second = rot(pair[0], 1, 1), rot(pair[1], 1, 1)
        return [first, jnp.where(lane == 0, first, second)]

    def right_of(pair):
        first, second = rot(pair[0], -1, 1), rot(pair[1], -1, 1)
        return [jnp.where(lane == LANES - 1, second, first), second]

    west = {}
    for name, res, val in (("e", res_e, v_e), ("o", res_o, v_o)):
        near_res, near_val = left_of(res), left_of(val)
        west[name] = [link(res[t], val[t], near_res[t], near_val[t]) for t in range(2)]
    east = {name: right_of(pair) for name, pair in west.items()}
    level = []
    coarse = []
    for t in range(2):
        v_in = link(res_e[t], v_e[t], res_o[t], v_o[t])
        v_up = link(res_e[t], v_e[t], rot(res_o[t], 1, 0), rot(v_o[t], 1, 0))
        v_dn = rot(v_up, -1, 0)
        we, wo, ee, eo = west["e"][t], west["o"][t], east["e"][t], east["o"][t]
        w_e = weights_of(g_e[t] + v_up + v_in + we + ee)
        w_o = weights_of(g_o[t] + v_in + v_dn + wo + eo)
        a_e = (1.0 - OMEGA) * v_e[t] + w_e * (v_in + jnp.where(odd, we, ee))
        a_o = (1.0 - OMEGA) * v_o[t] + w_o * (v_in + jnp.where(odd, wo, eo))
        b_e = w_e * jnp.where(odd, ee, we)
        b_o = w_o * jnp.where(odd, eo, wo)
        c_e = rot(w_e * v_up, -1, 0)
        c_o = rot(w_o * v_dn, 1, 0)
        p_es = rot(p_e[t], -1, 0)
        p_os = rot(p_o[t], 1, 0)
        terms = []
        for patch, own, side in ((p_e[t], a_e, b_e), (p_o[t], a_o, b_o), (p_es, c_e, None), (p_os, c_o, None)):
            spread = jnp.where(patch > 0, -0.125, 0.0)
            entry = [patch, 0.875 * own, spread * own]
            if side is not None:
                entry += [0.875 * side, spread * side]
            terms.append(entry)
        level.append((terms, w_e * v_e[t], w_o * v_o[t]))
        coarse.append((g_e[t] + g_o[t], v_up, we + wo))
    own_rows = slice(HALO // 2, n1 - HALO // 2)
    for index in (1, 2):
        moved = jnp.where(lane < LANES - HALO, rot(level[0][index], -HALO, 1), rot(level[1][index], -HALO, 1))
        w0_ref[index - 1] = moved[own_rows]

    m_in = selection(2 * LANES, lambda x, j: x // 2 == j)
    m_out = selection(2 * LANES, lambda x, j: x // 2 + 2 * (x % 2) - 1 == j)
    m_even = selection(2 * LANES, lambda x, j: x == 2 * j)
    m_both = jnp.concatenate([m_in, m_out], axis=0)

    def wide(index):
        return jnp.concatenate([coarse[0][index], coarse[1][index]], axis=1)

    zeros = jnp.zeros((c1_ref.shape[1] - n1, LANES), F32)
    c1_ref[0, 0:n1] = dot01(wide(0), m_in)
    c1_ref[1, 0:n1] = dot01(wide(1), m_in)
    c1_ref[2, 0:n1] = dot01(wide(2), m_even)
    for index in range(3):
        c1_ref[index, n1:] = zeros
    for k in range(RHS):
        parts_a = []
        parts_b = []
        for t in range(2):
            terms = level[t][0]
            tests = [entry[0] == k + 1.0 for entry in terms]
            picked = [jnp.where(test, entry[1], entry[2]) for test, entry in zip(tests, terms)]
            parts_a.append((picked[0] + picked[1]) + (picked[2] + picked[3]))
            parts_b.append(
                jnp.where(tests[0], terms[0][3], terms[0][4]) + jnp.where(tests[1], terms[1][3], terms[1][4])
            )
        r1_ref[k, 0:n1] = dot01(jnp.concatenate(parts_a + parts_b, axis=1), m_both)
        r1_ref[k, n1:] = zeros

    k_in = m_in[:LANES]
    k_out = m_out[:LANES]
    k_even = m_even[:LANES]
    k_both = jnp.concatenate([k_in, k_out], axis=0)
    l_in = selection(LANES, lambda x, j: x // 2 - 1 == j % 8)
    l_out = selection(LANES, lambda x, j: x // 2 + 2 * (x % 2) - 2 == j % 8)
    l_even = selection(LANES, lambda x, j: (x // 2 - 1 == j % 8) & (x % 2 == 0))
    l_both = jnp.concatenate([l_in, l_out], axis=0)
    for r_ref, c_ref, w_ref, next_r, next_c in (
        (r1_ref, c1_ref, w1_ref, r2_ref, c2_ref),
        (r2_ref, c2_ref, w2_ref, r3_ref, c3_ref),
        (r3_ref, c3_ref, w3_ref, None, None),
    ):
        half = r_ref.shape[1] // 2
        even, uneven = pl.ds(0, half, stride=2), pl.ds(1, half, stride=2)
        odd_lane = iota((half, LANES), 1) % 2 == 1
        ge, go = c_ref[0, even, :], c_ref[0, uneven, :]
        v_up, v_in = c_ref[1, even, :], c_ref[1, uneven, :]
        we, wo = c_ref[2, even, :], c_ref[2, uneven, :]
        ee, eo = rot(we, -1, 1), rot(wo, -1, 1)
        v_dn = rot(v_up, -1, 0)
        w_e = weights_of(ge + v_up + v_in + we + ee)
        w_o = weights_of(go + v_in + v_dn + wo + eo)
        a_e = (1.0 - OMEGA) + w_e * (v_in + jnp.where(odd_lane, we, ee))
        a_o = (1.0 - OMEGA) + w_o * (v_in + jnp.where(odd_lane, wo, eo))
        b_e = w_e * jnp.where(odd_lane, ee, we)
        b_o = w_o * jnp.where(odd_lane, eo, wo)
        c_e = w_e * v_up
        c_o = w_o * v_dn
        w_ref[0] = w_e
        w_ref[1] = w_o
        both, inner, evens = (k_both, k_in, k_even) if next_r is not None else (l_both, l_in, l_even)
        coarser = [dot01(ge + go, inner), dot01(v_up, inner), dot01(we + wo, evens)]
        fields = []
        for k in range(RHS):
            re, ro = r_ref[k, even, :], r_ref[k, uneven, :]
            own = a_e * re + a_o * ro + rot(c_o * ro, 1, 0) + rot(c_e * re, -1, 0)
            side = b_e * re + b_o * ro
            fields.append(dot01(jnp.concatenate([own, side], axis=1), both))
        if next_r is not None:
            for index in range(3):
                next_c[index] = coarser[index]
            for k in range(RHS):
                next_r[k] = fields[k]

    shape = fields[0].shape
    mine = iota(shape, 1) // 8 == iota(shape, 0) - 1

    def flat(field):
        return jnp.sum(jnp.where(mine, field, 0.0), axis=0, keepdims=True)

    sub = iota((8, LANES), 0)
    lane8 = iota((8, LANES), 1)
    links = jnp.where(sub < 4, flat(coarser[1]), flat(coarser[2]))
    turned = rot(links, 96, 1)
    for row in (1, 2):
        turned = jnp.where(sub % 4 == row, rot(links, 96 - 32 * row, 1), turned)
    tile = jnp.broadcast_to(flat(coarser[0]), (8, LANES))
    for k in range(RHS - 1):
        tile = jnp.where(sub == k, flat(fields[k]), tile)
    tile = jnp.where(lane8 < 96, tile, turned)

    @pl.loop(0, devices)
    def _(device):
        payload_ref[device] = tile


def up_kernel(own_ref, w0_ref, r1_ref, r2_ref, r3_ref, w1_ref, w2_ref, w3_ref, base_ref, t3_ref, t2_ref, t1_ref):
    spread = selection(LANES, lambda j, x: x // 2 == j)
    for r_ref, w_ref, coarse_ref, t_ref in (
        (r3_ref, w3_ref, None, t3_ref),
        (r2_ref, w2_ref, t3_ref, t2_ref),
        (r1_ref, w1_ref, t2_ref, t1_ref),
    ):
        half = w_ref.shape[1]
        for k in range(RHS):
            finer = None if coarse_ref is None else dot01(coarse_ref[k], spread)
            for index in range(2):
                rows = pl.ds(index, half, stride=2)
                smoothed = w_ref[index] * r_ref[k, rows, :]
                t_ref[k, rows, :] = smoothed if finer is None else finer + smoothed
    inner = selection(LANES, lambda j, x: j == x // 2 + HALO // 2)
    half = w0_ref.shape[1]
    sides = []
    for index in range(2):
        rows = pl.ds(index, half, stride=2)
        patch = own_ref[3, rows, :]
        weight = w0_ref[index]
        sides.append((rows, patch, 0.875 * weight, jnp.where(patch > 0, -0.125, 0.0) * weight))
    for k in range(RHS):
        finer = dot01(t1_ref[k, pl.ds(HALO // 2, half)], inner)
        for rows, patch, chosen, other in sides:
            base_ref[k, rows, :] = finer + jnp.where(patch == k + 1, chosen, other)


def solve_kernel(grid, all_ref, base_ref, out_ref, coef_ref, x_ref, r_ref, p_ref, q_ref, u_ref, done_ref, sem_ref):
    grid_rows, grid_cols = grid
    count = grid_rows * grid_cols
    lane = iota((8, LANES), 1)
    sub = iota((8, LANES), 0)
    inside = lane < 96

    def choose(test, yes, no):
        if isinstance(test, bool):
            return yes if test else no
        return jnp.where(test, yes, no)

    def every(body, init):
        if count <= 64:
            for tile in range(count):
                init = body(tile, init)
            return init
        return lax.fori_loop(0, count, body, init)

    def above(ref, t):
        return jnp.where(lane < 8, rot(ref[choose(t >= grid_cols, t - grid_cols, t)], 40, 1), rot(ref[t], 8, 1))

    def below(ref, t):
        near = ref[choose(t + grid_cols < count, t + grid_cols, t)]
        return jnp.where(lane >= 88, rot(near, 88, 1), rot(ref[t], 120, 1))

    def left(ref, t):
        near = ref[choose(t % grid_cols > 0, t - 1, t)]
        return jnp.where(lane % 8 == 0, rot(near, 121, 1), rot(ref[t], 1, 1))

    def right(ref, t):
        near = ref[choose(t % grid_cols < grid_cols - 1, t + 1, t)]
        return jnp.where(lane % 8 == 7, rot(near, 7, 1), rot(ref[t], 127, 1))

    def unpack(t, rr):
        tile = all_ref[t]
        known = jnp.where(inside & (sub < 7), tile, 0.0)
        rhs = jnp.where(sub < 7, known, -jnp.sum(known, axis=0, keepdims=True))
        r_ref[t] = rhs
        p_ref[t] = rhs
        coef_ref[0, t] = jnp.where(inside, jnp.broadcast_to(tile[7:8], (8, LANES)), 0.0)
        turned = jnp.zeros((8, LANES), F32)
        for row in range(3):
            turned = jnp.where((sub % 4 == row) & (lane // 32 == row), rot(tile, 32 * row + 32, 1), turned)
        north = jnp.sum(jnp.where(sub < 4, turned, 0.0), axis=0, keepdims=True)
        west = jnp.sum(jnp.where(sub < 4, 0.0, turned), axis=0, keepdims=True)
        coef_ref[1, t] = jnp.broadcast_to(north, (8, LANES))
        coef_ref[3, t] = jnp.broadcast_to(west, (8, LANES))
        return rr + rhs * rhs

    def total(values):
        return jnp.sum(values, axis=1, keepdims=True)

    zero = jnp.zeros((8, LANES), F32)
    rr = total(every(unpack, zero))

    def finish(t, carry):
        south = below(coef_ref.at[1], t)
        bottom = choose(t + grid_cols < count, 1.0, 0.0)
        south = jnp.where(lane < 88, south, jnp.where(inside, south * bottom, 0.0))
        east = right(coef_ref.at[3], t)
        last = choose(t % grid_cols < grid_cols - 1, 1.0, 0.0)
        east = jnp.where(inside, jnp.where(lane % 8 == 7, east * last, east), 0.0)
        coef_ref[2, t] = south
        coef_ref[4, t] = east
        coef_ref[0, t] = coef_ref[0, t] + coef_ref[1, t] + south + coef_ref[3, t] + east
        return carry

    every(finish, 0)

    def image_of(t, dot):
        here = p_ref[t]
        pulled = coef_ref[1, t] * above(p_ref, t) + coef_ref[2, t] * below(p_ref, t)
        pulled = pulled + coef_ref[3, t] * left(p_ref, t) + coef_ref[4, t] * right(p_ref, t)
        image = coef_ref[0, t] * here - pulled
        q_ref[t] = image
        return dot + here * image

    for sweep in range(ITERS):
        step = jnp.broadcast_to(rr / total(every(image_of, zero)), (8, LANES))

        def advance(t, norm):
            gain = step * p_ref[t]
            x_ref[t] = gain if sweep == 0 else x_ref[t] + gain
            if sweep + 1 == ITERS:
                return norm
            left_over = r_ref[t] - step * q_ref[t]
            r_ref[t] = left_over
            return norm + left_over * left_over

        norm = every(advance, zero)
        if sweep + 1 < ITERS:
            new = total(norm)
            ratio = jnp.broadcast_to(new / rr, (8, LANES))
            rr = new

            def turn(t, carry):
                p_ref[t] = r_ref[t] + ratio * p_ref[t]
                return carry

            every(turn, 0)

    mine = x_ref[lax.axis_index("row") * grid_cols + lax.axis_index("col")]
    groups = u_ref.shape[0] // 8
    stacked = jnp.concatenate([jnp.where(lane // 8 == i, mine, 0.0) for i in range(groups)], axis=0)
    widen = selection(LANES, lambda x, j: x % 8 == j // HALO)
    u_ref[...] = dot01(stacked, widen)
    copies = []
    for k in range(RHS):
        for i in range(groups):
            rows = pl.ds(HALO * i, HALO)
            done_ref[k, rows, :] = base_ref[k, rows, :] + u_ref[pl.ds(8 * i + k, 1), :]
        copy = pltpu.make_async_copy(done_ref.at[k], out_ref.at[k], sem_ref.at[k])
        copy.start()
        copies.append(copy)
    for copy in copies:
        copy.wait()


def exchanged(first, second, axis, other):
    sizes = {name: lax.axis_size(name) for name in (axis, other)}

    def pairs(step):
        found = []
        for i in range(sizes["row"]):
            for j in range(sizes["col"]):
                place = {"row": i, "col": j}
                target = dict(place)
                at = place[axis]
                if step == 0:
                    target[axis] = at ^ 1
                elif at in (0, sizes[axis] - 1):
                    target[other] = place[other] ^ 1
                else:
                    target[axis] = at + 1 if at % 2 else at - 1
                found.append((i * sizes["col"] + j, target["row"] * sizes["col"] + target["col"]))
        return found

    return [lax.ppermute(part, ("row", "col"), pairs(step)) for step, part in enumerate((first, second))]


def shards(resistance, ground, nodata, patch_ids):
    grid = (lax.axis_size("row"), lax.axis_size("col"))
    devices = grid[0] * grid[1]
    rows, cols = resistance.shape
    own = [pltpu.with_memory_space_constraint(part, pltpu.HBM) for part in (resistance, ground, nodata, patch_ids)]
    def near(value):
        return pltpu.with_memory_space_constraint(value, pltpu.VMEM)

    def call(kernel, outs, scratch, *args, **options):
        outs = tuple(pltpu.VMEM(out, F32) for out in outs)
        scratch = [pltpu.VMEM(part, F32) if isinstance(part, tuple) else part for part in scratch]
        name = kernel.__name__
        params = pltpu.CompilerParams(vmem_limit_bytes=VMEM_LIMIT)
        return pl.pallas_call(
            kernel, out_shape=outs, scratch_shapes=scratch, name=name, compiler_params=params, **options
        )(*args)

    def all_near(values):
        return [near(value) for value in values]

    strip = (4 * HALO, cols)
    kept, first, second = call(
        pack_rows_kernel,
        [(4, rows, cols), strip, strip],
        [pltpu.VMEM((rows, cols), jnp.int32)] * 2 + [pltpu.SemaphoreType.DMA((4,))],
        *own,
        in_specs=[pl.BlockSpec(memory_space=pltpu.HBM)] * 4,
    )
    first, second = exchanged(first, second, "row", "col")
    tall_rows = rows + 2 * HALO
    strip = (tall_rows // 2, LANES)
    kept = near(kept)
    tall, first, second = call(
        pack_cols_kernel, [(4, tall_rows, cols), strip, strip], [], kept, near(first), near(second)
    )
    first, second = exchanged(first, second, "col", "row")
    sizes = [128, 64, 32]
    payload, w0, *levels = call(
        down_kernel,
        [(devices, 8, LANES), (2, rows // 2, LANES)]
        + [(RHS, size, LANES) for size in sizes]
        + [(2, size // 2, LANES) for size in sizes],
        [(8, tall_rows, LANES)] + [(3, size, LANES) for size in sizes],
        *all_near((tall, first, second)),
    )
    everything = near(lax.all_to_all(payload, ("row", "col"), 0, 0))
    (base,) = call(
        up_kernel,
        [(RHS, rows, cols)],
        [(RHS, size, LANES) for size in sizes[::-1]],
        kept,
        *all_near([w0] + levels),
        cost_estimate=pl.CostEstimate(flops=10**8, bytes_accessed=10**6, transcendentals=0),
    )
    field = pltpu.VMEM((devices, 8, LANES), F32)
    return pl.pallas_call(
        functools.partial(solve_kernel, grid),
        out_shape=jax.ShapeDtypeStruct((RHS, rows, cols), F32),
        out_specs=pl.BlockSpec(memory_space=pl.ANY),
        scratch_shapes=[pltpu.VMEM((5, devices, 8, LANES), F32)]
        + [field] * 4
        + [pltpu.VMEM((rows // HALO * 8, LANES), F32), pltpu.VMEM((RHS, rows, cols), F32)]
        + [pltpu.SemaphoreType.DMA((RHS,))],
        compiler_params=pltpu.CompilerParams(vmem_limit_bytes=VMEM_LIMIT),
        name="solve_kernel",
    )(everything, near(base))


def solution(mesh):
    spec = P("row", "col")
    return jax.shard_map(shards, mesh=mesh, in_specs=(spec,) * 4, out_specs=P(None, "row", "col"), check_vma=False)
```

```python
import functools

import jax
import jax.numpy as jnp
from jax import lax
from jax.experimental import pallas as pl
from jax.experimental.pallas import tpu as pltpu
from jax.sharding import PartitionSpec as P

RHS = 8
ITERS = 4
OMEGA = 0.8
HALO = 16
LANES = 128
F32 = jnp.float32
BF16 = jnp.bfloat16
PIECES = 2
VMEM_LIMIT = 32 * 2**20


def iota(shape, dim):
    return lax.broadcasted_iota(jnp.int32, shape, dim)


def selection(rows, test):
    shape = (rows, LANES)
    return jnp.where(test(iota(shape, 0), iota(shape, 1)), 1.0, 0.0).astype(BF16)


def split(values):
    pieces = []
    for piece in range(PIECES):
        pieces.append(values.astype(BF16))
        if piece + 1 < PIECES:
            values = values - pieces[-1].astype(F32)
    return pieces


def stacked(matrix):
    return jnp.concatenate([matrix] * PIECES, axis=0)


def dot01(parts, matrix):
    pieces = [split(part) for part in parts]
    rows = jnp.concatenate([piece[i] for i in range(PIECES) for piece in pieces], axis=1)
    return jnp.dot(rows, matrix, preferred_element_type=F32)


def rot(values, shift, axis):
    return pltpu.roll(values, shift % values.shape[axis], axis)


def column(x):
    return jnp.where(x < 16, x + 1, x + 127)


def outward(x):
    return x // 2 + 2 * (x % 2) - 1


def turn_test(first):
    def test(x, j):
        y = x - 64 * first
        own = (y >= 0) & (y < 32) & (column(y) // 2 == j)
        return own | ((y >= 32) & (y < 64) & (outward(column(y - 32)) == j))

    return test


def level_tests(shift, places):
    m_in = lambda x, j: x // 2 - shift == j % places
    m_out = lambda x, j: outward(x) - shift == j % places
    m_even = lambda x, j: (x // 2 - shift == j % places) & (x % 2 == 0)
    return [[m_in, m_out], [m_in], [m_even]]


TABLES = (
    [
        [lambda c, j: (c + HALO) // 2 == j, lambda c, j: outward(c + HALO) == j],
        [lambda c, j: (c + HALO) // 2 == j],
        [lambda c, j: (c + HALO == 2 * j) & (c > 0)],
        [lambda x, j: (x < 32) & (x != 15) & (x != 16) & (column(x) // 2 == j)],
        [lambda x, j: (x < 32) & (column(x) == 2 * j)],
        [turn_test(0)],
        [turn_test(1)],
    ]
    + level_tests(0, LANES)
    + level_tests(1, 8)
    + [
        [lambda j, x: x // 2 == j],
        [lambda j, x: j == x // 2 + HALO // 2],
        [lambda x, j: x % 8 == j // HALO],
    ]
)


def tables_kernel(own_ref, *out_refs):
    for tests, out_ref in zip(TABLES, out_refs):
        out_ref[...] = stacked(jnp.concatenate([selection(LANES, test) for test in tests], axis=0))


def pack_rows_kernel(
    res_ref, ground_ref, nodata_ref, patch_ref, own_ref, first_ref, second_ref, nodata_near_ref, patch_near_ref, sem_ref
):
    rows = res_ref.shape[0]
    copies = [
        pltpu.make_async_copy(source, target, sem_ref.at[which])
        for which, (source, target) in enumerate(
            (
                (res_ref, own_ref.at[0]),
                (ground_ref, own_ref.at[1]),
                (nodata_ref, nodata_near_ref),
                (patch_ref, patch_near_ref),
            )
        )
    ]
    for copy in copies:
        copy.start()
    for copy in copies:
        copy.wait()
    own_ref[2] = jnp.where(nodata_near_ref[...] == 0, 1.0, 0.0)
    own_ref[3] = patch_near_ref[...].astype(F32)
    odd = lax.axis_index("row") % 2 == 1
    for which in range(4):
        top = own_ref[which, :HALO]
        bottom = own_ref[which, rows - HALO :]
        part = pl.ds(which * HALO, HALO)
        first_ref[part] = jnp.where(odd, top, bottom)
        second_ref[part] = jnp.where(odd, bottom, top)


def before_after(axis, first, second):
    index = lax.axis_index(axis)
    odd = index % 2 == 1
    before = jnp.where(index > 0, jnp.where(odd, first, second), 0.0)
    after = jnp.where(index < lax.axis_size(axis) - 1, jnp.where(odd, second, first), 0.0)
    return before, after


def pack_cols_kernel(own_ref, from_first_ref, from_second_ref, order_ref, tall_ref, first_ref, second_ref):
    half = own_ref.shape[1] // 2
    shape = first_ref.shape
    group_of = iota(shape, 1) // HALO
    odd = lax.axis_index("col") % 2 == 1
    above, below = before_after("row", from_first_ref[...], from_second_ref[...])
    to_right = jnp.zeros(shape, F32)
    to_left = jnp.zeros(shape, F32)
    for which in range(4):
        part = slice(which * HALO, which * HALO + HALO)
        upper = jnp.concatenate([above[part], own_ref[which, :half]], axis=0)
        lower = jnp.concatenate([own_ref[which, half:], below[part]], axis=0)
        if which < 2:
            upper = jnp.where(upper > 0, upper, 1.0)
            lower = jnp.where(lower > 0, lower, 1.0)
        tall_ref[which, : half + HALO] = upper
        tall_ref[which, half + HALO :] = lower
        for side, values in enumerate((upper, lower)):
            group = 2 * which + side
            here = group_of == group
            to_right = jnp.where(here, rot(values, HALO * group + HALO, 1), to_right)
            to_left = jnp.where(here, rot(values, HALO * group, 1), to_left)
    first_ref[...] = jnp.where(odd, to_left, to_right)
    second_ref[...] = jnp.where(odd, to_right, to_left)


def link(resist, validity, near_resist, near_valid):
    return (validity * near_valid) * (2.0 / (resist + near_resist))


def weights_of(diag):
    return OMEGA / jnp.where(diag > 0, diag, 1.0)


def level_0(fields, odd_column, west, east):
    res, ground, val, patch = fields
    link_w = [west(res[i], val[i], i) for i in range(2)]
    link_e = [east(link_w[i], i) for i in range(2)]
    v_in = link(res[0], val[0], res[1], val[1])
    v_up = link(res[0], val[0], rot(res[1], 1, 0), rot(val[1], 1, 0))
    v_dn = rot(v_up, -1, 0)
    vertical = (v_up, v_dn)
    weight, own, side, away = [], [], [], []
    for i in range(2):
        w = weights_of(ground[i] + v_in + vertical[i] + link_w[i] + link_e[i])
        own.append((1.0 - OMEGA) * val[i] + w * (v_in + jnp.where(odd_column, link_w[i], link_e[i])))
        side.append(w * jnp.where(odd_column, link_e[i], link_w[i]))
        away.append(w * vertical[i])
        weight.append(w * val[i])
    away = [rot(away[0], -1, 0), rot(away[1], 1, 0)]
    return weight, own, side, away, link_w, v_up


def choices(patch, values):
    spread = jnp.where(patch > 0, -0.125, 0.0)
    return [(0.875 * value, spread * value) for value in values]


def pick(test, choice):
    return jnp.where(test, choice[0], choice[1])


def rows_by_parity(ref, which):
    half = ref.shape[1] // 2
    return [ref[which, pl.ds(start, half, stride=2), :] for start in range(2)]


def inner_kernel(tall_ref, both_ref, sum_ref, even_ref, r1_ref, c1_ref, w0_ref, edge_ref, west_ref):
    half = tall_ref.shape[1] // 2
    lane = iota((half, LANES), 1)
    fields = [rows_by_parity(tall_ref, which) for which in range(4)]
    patch = fields[3]
    odd = lane % 2 == 1
    weight, own, side, away, west, v_up = level_0(
        fields,
        odd,
        lambda res, val, i: link(res, val, rot(res, 1, 1), rot(val, 1, 1)),
        lambda value, i: rot(value, -1, 1),
    )
    inside = (lane > 0) & (lane < LANES - 1)
    own, side, away = ([jnp.where(inside, value, 0.0) for value in pair] for pair in (own, side, away))
    kept = slice(HALO // 2, half - HALO // 2)
    for i in range(2):
        w0_ref[i] = weight[i][kept]
        west_ref[i] = jnp.where(lane == 15, rot(west[i], 14, 1), rot(west[i], 17, 1))
    whole_lane = iota((2 * half, LANES), 1)
    for which in range(4):
        value = tall_ref[which]
        edge_ref[which] = jnp.where(whole_lane == 15, rot(value, 15, 1), rot(value, 17, 1))
    c1_ref[0] = dot01([fields[1][0] + fields[1][1]], sum_ref[...])
    c1_ref[1] = dot01([v_up], sum_ref[...])
    c1_ref[2] = dot01([west[0] + west[1]], even_ref[...])
    near = [choices(patch[i], (own[i], side[i])) for i in range(2)]
    patch_away = [rot(patch[0], -1, 0), rot(patch[1], 1, 0)]
    far = [choices(patch_away[i], (away[i],)) for i in range(2)]
    for k in range(RHS - 1):
        tests = [patch[i] == k + 1.0 for i in range(2)]
        tests_away = [patch_away[i] == k + 1.0 for i in range(2)]
        to_own = pick(tests[0], near[0][0]) + pick(tests[1], near[1][0])
        to_own = to_own + (pick(tests_away[0], far[0][0]) + pick(tests_away[1], far[1][0]))
        to_side = pick(tests[0], near[0][1]) + pick(tests[1], near[1][1])
        r1_ref[k] = dot01([to_own, to_side], both_ref[...])


def down_kernel(
    from_first_ref,
    from_second_ref,
    r1_inner_ref,
    c1_inner_ref,
    w0_inner_ref,
    edge_ref,
    west_ref,
    sum_ref,
    even_ref,
    turn_first_ref,
    turn_second_ref,
    usual_both_ref,
    usual_sum_ref,
    usual_even_ref,
    last_both_ref,
    last_sum_ref,
    last_even_ref,
    payload_ref,
    w0_ref,
    r1_ref,
    r2_ref,
    r3_ref,
    w1_ref,
    w2_ref,
    w3_ref,
    ext_ref,
    c1_ref,
    c2_ref,
    c3_ref,
):
    devices = payload_ref.shape[0]
    n1 = edge_ref.shape[1] // 2
    lane = iota((n1, LANES), 1)
    from_left, from_right = before_after("col", from_first_ref[...], from_second_ref[...])
    at_left = (lane < 15) | (lane == LANES - 1)
    at_edge = (lane == 15) | (lane == 16)
    at_right = (lane > 16) & (lane < 33)
    for which in range(4):
        for part in range(2):
            group = 2 * which + part
            rows = pl.ds(part * n1, n1)
            value = jnp.where(at_right, rot(from_right, 17 - HALO * group, 1), 0.0)
            value = jnp.where(at_left, rot(from_left, -1 - HALO * group, 1), value)
            value = jnp.where(at_edge, edge_ref[which, rows, :], value)
            if which < 2:
                value = jnp.where(value > 0, value, 1.0)
            ext_ref[which, rows, :] = value
    fields = [rows_by_parity(ext_ref, which) for which in range(4)]
    weight, own, side, away, west, v_up = level_0(
        fields,
        lane % 2 == 0,
        lambda res, val, i: jnp.where(
            lane == 16, west_ref[i], link(res, val, rot(res, 1, 1), rot(val, 1, 1))
        ),
        lambda value, i: jnp.where(lane == 15, west_ref[i], rot(value, -1, 1)),
    )
    kept = slice(HALO // 2, n1 - HALO // 2)
    for i in range(2):
        value = weight[i][kept]
        full = iota(value.shape, 1)
        w0_ref[i] = jnp.where(
            full == 0, value[:, 15:16], jnp.where(full == LANES - 1, value[:, 16:17], w0_inner_ref[i])
        )

    zeros = jnp.zeros((c1_ref.shape[1] - n1, LANES), F32)
    c1_ref[0, 0:n1] = c1_inner_ref[0] + dot01([fields[1][0] + fields[1][1]], sum_ref[...])
    c1_ref[1, 0:n1] = c1_inner_ref[1] + dot01([v_up], sum_ref[...])
    c1_ref[2, 0:n1] = c1_inner_ref[2] + dot01([west[0] + west[1]], even_ref[...])
    for index in range(3):
        c1_ref[index, n1:] = zeros

    outer = lane < 32

    def twice(value):
        return value + rot(value, 64, 1)

    own, side, away, patch = (
        [jnp.where(outer, value, 0.0) for value in pair] for pair in (own, side, away, fields[3])
    )
    patch = [value + rot(value, 32, 1) for value in patch]
    later = jnp.where(lane >= 64, 1.0, 0.0)
    patch = [twice(value) for value in patch]
    both = [twice(own[i] + rot(side[i], 32, 1)) for i in range(2)]
    away = [twice(value) for value in away]
    patch_away = [rot(patch[0], -1, 0), rot(patch[1], 1, 0)]
    terms = []
    for value, entry in ((patch[0], both[0]), (patch[1], both[1]), (patch_away[0], away[0]), (patch_away[1], away[1])):
        terms.append((value - later, choices(value, (entry,))[0]))

    turns = (turn_first_ref, turn_second_ref)
    for first in range(0, RHS, 2):
        picked = [pick(value == first + 1.0, choice) for value, choice in terms]
        outer_part = (picked[0] + picked[1]) + (picked[2] + picked[3])
        for k in range(first, min(first + 2, RHS - 1)):
            r1_ref[k, 0:n1] = r1_inner_ref[k] + dot01([outer_part], turns[k - first][...])
            r1_ref[k, n1:] = zeros

    usual = (usual_both_ref, usual_sum_ref, usual_even_ref)
    last = (last_both_ref, last_sum_ref, last_even_ref)
    for r_ref, c_ref, w_ref, next_r, next_c in (
        (r1_ref, c1_ref, w1_ref, r2_ref, c2_ref),
        (r2_ref, c2_ref, w2_ref, r3_ref, c3_ref),
        (r3_ref, c3_ref, w3_ref, None, None),
    ):
        half = r_ref.shape[1] // 2
        even, uneven = pl.ds(0, half, stride=2), pl.ds(1, half, stride=2)
        odd_lane = iota((half, LANES), 1) % 2 == 1
        ge, go = c_ref[0, even, :], c_ref[0, uneven, :]
        v_up, v_in = c_ref[1, even, :], c_ref[1, uneven, :]
        we, wo = c_ref[2, even, :], c_ref[2, uneven, :]
        ee, eo = rot(we, -1, 1), rot(wo, -1, 1)
        v_dn = rot(v_up, -1, 0)
        w_e = weights_of(ge + v_up + v_in + we + ee)
        w_o = weights_of(go + v_in + v_dn + wo + eo)
        a_e = (1.0 - OMEGA) + w_e * (v_in + jnp.where(odd_lane, we, ee))
        a_o = (1.0 - OMEGA) + w_o * (v_in + jnp.where(odd_lane, wo, eo))
        b_e = w_e * jnp.where(odd_lane, ee, we)
        b_o = w_o * jnp.where(odd_lane, eo, wo)
        c_e = w_e * v_up
        c_o = w_o * v_dn
        w_ref[0] = w_e
        w_ref[1] = w_o
        both, inner, evens = (table[...] for table in (usual if next_r is not None else last))
        coarser = [dot01([ge + go], inner), dot01([v_up], inner), dot01([we + wo], evens)]
        fields = []
        for k in range(RHS - 1):
            re, ro = r_ref[k, even, :], r_ref[k, uneven, :]
            own = a_e * re + a_o * ro + rot(c_o * ro, 1, 0) + rot(c_e * re, -1, 0)
            side = b_e * re + b_o * ro
            fields.append(dot01([own, side], both))
        if next_r is not None:
            for index in range(3):
                next_c[index] = coarser[index]
            for k in range(RHS - 1):
                next_r[k] = fields[k]

    shape = fields[0].shape
    mine = iota(shape, 1) // 8 == iota(shape, 0) - 1

    def flat(field):
        return jnp.sum(jnp.where(mine, field, 0.0), axis=0, keepdims=True)

    sub = iota((8, LANES), 0)
    lane8 = iota((8, LANES), 1)
    links = jnp.where(sub < 4, flat(coarser[1]), flat(coarser[2]))
    turned = rot(links, 96, 1)
    for row in (1, 2):
        turned = jnp.where(sub % 4 == row, rot(links, 96 - 32 * row, 1), turned)
    tile = jnp.broadcast_to(flat(coarser[0]), (8, LANES))
    for k in range(RHS - 1):
        tile = jnp.where(sub == k, flat(fields[k]), tile)
    tile = jnp.where(lane8 < 96, tile, turned)

    @pl.loop(0, devices)
    def _(device):
        payload_ref[device] = tile


def up_kernel(
    own_ref,
    w0_ref,
    r1_ref,
    r2_ref,
    r3_ref,
    w1_ref,
    w2_ref,
    w3_ref,
    spread_ref,
    finest_ref,
    base_ref,
    t3_ref,
    t2_ref,
    t1_ref,
):
    for r_ref, w_ref, coarse_ref, t_ref in (
        (r3_ref, w3_ref, None, t3_ref),
        (r2_ref, w2_ref, t3_ref, t2_ref),
        (r1_ref, w1_ref, t2_ref, t1_ref),
    ):
        half = w_ref.shape[1]
        for k in range(RHS - 1):
            finer = None if coarse_ref is None else dot01([coarse_ref[k]], spread_ref[...])
            for index in range(2):
                rows = pl.ds(index, half, stride=2)
                smoothed = w_ref[index] * r_ref[k, rows, :]
                t_ref[k, rows, :] = smoothed if finer is None else finer + smoothed
    half = w0_ref.shape[1]
    sides = []
    for index in range(2):
        rows = pl.ds(index, half, stride=2)
        patch = own_ref[3, rows, :]
        sides.append((rows, patch, choices(patch, (w0_ref[index],))[0]))
    left_over = None
    for k in range(RHS):
        if k + 1 < RHS:
            coarse = t1_ref[k, pl.ds(HALO // 2, half)]
            left_over = -coarse if left_over is None else left_over - coarse
        else:
            coarse = left_over
        finer = dot01([coarse], finest_ref[...])
        for rows, patch, choice in sides:
            base_ref[k, rows, :] = finer + pick(patch == k + 1.0, choice)


def solve_kernel(
    grid,
    all_ref,
    base_ref,
    widen_ref,
    out_ref,
    coef_ref,
    x_ref,
    r_ref,
    q_ref,
    p_ref,
    p_up_ref,
    p_down_ref,
    p_first_ref,
    p_last_ref,
    u_ref,
    done_ref,
    sem_ref,
):
    grid_rows, grid_cols = grid
    count = grid_rows * grid_cols
    lane = iota((8, LANES), 1)
    column = lane % 8

    def choose(test, yes, no):
        if isinstance(test, bool):
            return yes if test else no
        return jnp.where(test, yes, no)

    def at(t):
        return pl.ds(8 * t if isinstance(t, int) else pl.multiple_of(8 * t, 8), 8)

    def every(body, init):
        if count <= 64:
            for tile in range(count):
                init = body(tile, init)
            return init
        return lax.fori_loop(0, count, body, init)

    all_lane = iota((count, LANES), 1)
    inside = all_lane < 96
    rows = [all_ref[pl.ds(i, count, stride=8), :] for i in range(8)]
    north, west = (
        jnp.where(
            all_lane < 32,
            rot(rows[i], 32, 1),
            jnp.where(all_lane < 64, rot(rows[i + 1], 64, 1), rot(rows[i + 2], 96, 1)),
        )
        for i in (0, 4)
    )
    north, west = jnp.where(inside, north, 0.0), jnp.where(inside, west, 0.0)
    north_below = jnp.concatenate([north[grid_cols:], jnp.zeros((grid_cols, LANES), F32)], axis=0)
    south = jnp.where(all_lane >= 88, rot(north_below, 88, 1), rot(north, 120, 1))
    west_right = jnp.where(iota((count, LANES), 0) % grid_cols < grid_cols - 1, rot(west, -1, 0), 0.0)
    east = jnp.where(all_lane % 8 == 7, rot(west_right, 7, 1), rot(west, 127, 1))
    south, east = jnp.where(inside, south, 0.0), jnp.where(inside, east, 0.0)
    coef_ref[0] = jnp.where(inside, rows[7], 0.0) + north + south + west + east
    coef_ref[1] = north
    coef_ref[2] = south
    coef_ref[3] = west
    coef_ref[4] = east
    others = ((rows[0] + rows[1]) + (rows[2] + rows[3])) + ((rows[4] + rows[5]) + rows[6])
    r_ref[...] = jnp.where(iota(r_ref.shape, 1) < 96, all_ref[...], 0.0)
    r_ref[pl.ds(7, count, stride=8), :] = jnp.where(inside, -others, 0.0)

    def total(values):
        return jnp.sum(values, axis=1, keepdims=True)

    def direct(t, values):
        p_ref[at(t), :] = values
        p_up_ref[at(t), :] = rot(values, 8, 1)
        p_down_ref[at(t), :] = rot(values, 120, 1)
        p_last_ref[at(t), :] = rot(values, 40, 1)
        p_first_ref[at(t), :] = rot(values, 88, 1)

    def begin(t, norm):
        values = r_ref[at(t), :]
        direct(t, values)
        return norm + values * values

    zero = jnp.zeros((8, LANES), F32)
    rr = total(every(begin, zero))

    def image_of(t, dot):
        here = p_ref[at(t), :]
        up = p_last_ref[at(choose(t >= grid_cols, t - grid_cols, t)), :]
        down = p_first_ref[at(choose(t + grid_cols < count, t + grid_cols, t)), :]
        left = p_down_ref[at(choose(t % grid_cols > 0, t - 1, t)), :]
        right = p_up_ref[at(choose(t % grid_cols < grid_cols - 1, t + 1, t)), :]
        up = jnp.where(lane < 8, up, p_up_ref[at(t), :])
        down = jnp.where(lane >= 88, down, p_down_ref[at(t), :])
        left = rot(jnp.where(column == 7, left, here), 1, 1)
        right = rot(jnp.where(column == 0, right, here), -1, 1)
        pulled = coef_ref[1, pl.ds(t, 1), :] * up + coef_ref[2, pl.ds(t, 1), :] * down
        pulled = pulled + coef_ref[3, pl.ds(t, 1), :] * left + coef_ref[4, pl.ds(t, 1), :] * right
        image = coef_ref[0, pl.ds(t, 1), :] * here - pulled
        q_ref[at(t), :] = image
        return dot + here * image

    for sweep in range(ITERS - 1):
        step = jnp.broadcast_to(rr / total(every(image_of, zero)), (8, LANES))

        def advance(t, norm):
            left_over = r_ref[at(t), :] - step * q_ref[at(t), :]
            r_ref[at(t), :] = left_over
            return norm + left_over * left_over

        new = total(every(advance, zero))
        ratio = jnp.broadcast_to(new / rr, (8, LANES))
        rr = new

        def turn(t, carry):
            values = p_ref[at(t), :]
            gain = step * values
            x_ref[at(t), :] = gain if sweep == 0 else x_ref[at(t), :] + gain
            direct(t, r_ref[at(t), :] + ratio * values)
            return carry

        every(turn, 0)

    step = jnp.broadcast_to(rr / total(every(image_of, zero)), (8, LANES))
    device = lax.axis_index("row") * grid_cols + lax.axis_index("col")
    mine = x_ref[at(device), :] + step * p_ref[at(device), :]
    groups = u_ref.shape[0] // 8
    placed = jnp.concatenate([jnp.where(lane // 8 == i, mine, 0.0) for i in range(groups)], axis=0)
    u_ref[...] = dot01([placed], widen_ref[...])
    copies = []
    for k in range(RHS):
        for i in range(groups):
            rows = pl.ds(HALO * i, HALO)
            done_ref[k, rows, :] = base_ref[k, rows, :] + u_ref[pl.ds(8 * i + k, 1), :]
        copy = pltpu.make_async_copy(done_ref.at[k], out_ref.at[k], sem_ref.at[k])
        copy.start()
        copies.append(copy)
    for copy in copies:
        copy.wait()


def exchanged(first, second, axis, other):
    sizes = {name: lax.axis_size(name) for name in (axis, other)}

    def pairs(step):
        found = []
        for i in range(sizes["row"]):
            for j in range(sizes["col"]):
                place = {"row": i, "col": j}
                target = dict(place)
                at = place[axis]
                if step == 0:
                    target[axis] = at ^ 1
                elif at in (0, sizes[axis] - 1):
                    target[other] = place[other] ^ 1
                else:
                    target[axis] = at + 1 if at % 2 else at - 1
                found.append((i * sizes["col"] + j, target["row"] * sizes["col"] + target["col"]))
        return found

    return [lax.ppermute(part, ("row", "col"), pairs(step)) for step, part in enumerate((first, second))]


def shards(resistance, ground, nodata, patch_ids):
    grid = (lax.axis_size("row"), lax.axis_size("col"))
    devices = grid[0] * grid[1]
    rows, cols = resistance.shape
    own = [pltpu.with_memory_space_constraint(part, pltpu.HBM) for part in (resistance, ground, nodata, patch_ids)]
    def near(value):
        return pltpu.with_memory_space_constraint(value, pltpu.VMEM)

    def call(kernel, outs, scratch, *args, **options):
        outs = tuple(pltpu.VMEM(out, F32) if isinstance(out, tuple) else out for out in outs)
        scratch = [pltpu.VMEM(part, F32) if isinstance(part, tuple) else part for part in scratch]
        name = kernel.__name__
        params = pltpu.CompilerParams(vmem_limit_bytes=VMEM_LIMIT)
        return pl.pallas_call(
            kernel, out_shape=outs, scratch_shapes=scratch, name=name, compiler_params=params, **options
        )(*args)

    def all_near(values):
        return [near(value) for value in values]

    strip = (4 * HALO, cols)
    kept, first, second = call(
        pack_rows_kernel,
        [(4, rows, cols), strip, strip],
        [pltpu.VMEM((rows, cols), jnp.int32)] * 2 + [pltpu.SemaphoreType.DMA((4,))],
        *own,
        in_specs=[pl.BlockSpec(memory_space=pltpu.HBM)] * 4,
    )
    first, second = exchanged(first, second, "row", "col")
    tall_rows = rows + 2 * HALO
    strip = (tall_rows // 2, LANES)
    kept = near(kept)
    tables = all_near(
        call(
            tables_kernel,
            [pltpu.VMEM((PIECES * LANES * len(tests), LANES), BF16) for tests in TABLES],
            [],
            kept,
            cost_estimate=pl.CostEstimate(flops=10**7, bytes_accessed=10**6, transcendentals=0),
        )
    )
    tall, first, second = call(
        pack_cols_kernel, [(4, tall_rows, cols), strip, strip], [], kept, near(first), near(second), tables[0]
    )
    first, second = exchanged(first, second, "col", "row")
    sizes = [128, 64, 32]
    n1 = tall_rows // 2
    inner = call(
        inner_kernel,
        [(RHS - 1, n1, LANES), (3, n1, LANES), (2, rows // 2, LANES), (4, tall_rows, LANES), (2, n1, LANES)],
        [],
        near(tall),
        *tables[:3],
        cost_estimate=pl.CostEstimate(flops=10**8, bytes_accessed=10**6, transcendentals=0),
    )
    payload, w0, *levels = call(
        down_kernel,
        [(devices, 8, LANES), (2, rows // 2, LANES)]
        + [(RHS - 1, size, LANES) for size in sizes]
        + [(2, size // 2, LANES) for size in sizes],
        [(4, tall_rows, LANES)] + [(3, size, LANES) for size in sizes],
        *all_near((first, second, *inner)),
        *tables[3:13],
    )
    everything = lax.all_to_all(payload, ("row", "col"), 0, 0)
    (base,) = call(
        up_kernel,
        [(RHS, rows, cols)],
        [(RHS - 1, size, LANES) for size in sizes[::-1]],
        kept,
        *all_near([w0] + levels),
        *tables[13:15],
        cost_estimate=pl.CostEstimate(flops=10**8, bytes_accessed=10**6, transcendentals=0),
    )
    return pl.pallas_call(
        functools.partial(solve_kernel, grid),
        out_shape=jax.ShapeDtypeStruct((RHS, rows, cols), F32),
        out_specs=pl.BlockSpec(memory_space=pl.ANY),
        scratch_shapes=[pltpu.VMEM((5, devices, LANES), F32)]
        + [pltpu.VMEM((devices * 8, LANES), F32)] * 8
        + [pltpu.VMEM((rows // HALO * 8, LANES), F32), pltpu.VMEM((RHS, rows, cols), F32)]
        + [pltpu.SemaphoreType.DMA((RHS,))],
        compiler_params=pltpu.CompilerParams(vmem_limit_bytes=VMEM_LIMIT),
        name="solve_kernel",
    )(near(everything.reshape(devices * 8, LANES)), near(base), tables[15])


def solution(mesh):
    spec = P("row", "col")
    return jax.shard_map(shards, mesh=mesh, in_specs=(spec,) * 4, out_specs=P(None, "row", "col"), check_vma=False)
```

```python
import functools

import jax
import jax.numpy as jnp
from jax import lax
from jax.experimental import pallas as pl
from jax.experimental.pallas import tpu as pltpu
from jax.sharding import PartitionSpec as P

RHS = 8
ITERS = 4
OMEGA = 0.8
HALO = 16
LANES = 128
F32 = jnp.float32
BF16 = jnp.bfloat16
PIECES = 2
VMEM_LIMIT = 32 * 2**20


def iota(shape, dim):
    return lax.broadcasted_iota(jnp.int32, shape, dim)


def selection(rows, test):
    shape = (rows, LANES)
    return jnp.where(test(iota(shape, 0), iota(shape, 1)), 1.0, 0.0).astype(BF16)


def split(values):
    pieces = []
    for piece in range(PIECES):
        pieces.append(values.astype(BF16))
        if piece + 1 < PIECES:
            values = values - pieces[-1].astype(F32)
    return pieces


def stacked(matrix):
    return jnp.concatenate([matrix] * PIECES, axis=0)


def dot01(parts, matrix):
    pieces = [split(part) for part in parts]
    rows = jnp.concatenate([piece[i] for i in range(PIECES) for piece in pieces], axis=1)
    return jnp.dot(rows, matrix, preferred_element_type=F32)


def rot(values, shift, axis):
    return pltpu.roll(values, shift % values.shape[axis], axis)


def column(x):
    return jnp.where(x < 16, x + 1, x + 127)


def outward(x):
    return x // 2 + 2 * (x % 2) - 1


def turn_test(first):
    def test(x, j):
        y = x - 64 * first
        own = (y >= 0) & (y < 32) & (column(y) // 2 == j)
        return own | ((y >= 32) & (y < 64) & (outward(column(y - 32)) == j))

    return test


def level_tests(shift, places):
    m_in = lambda x, j: x // 2 - shift == j % places
    m_out = lambda x, j: outward(x) - shift == j % places
    m_even = lambda x, j: (x // 2 - shift == j % places) & (x % 2 == 0)
    return [[m_in, m_out], [m_in], [m_even]]


TABLES = (
    [
        [lambda c, j: (c + HALO) // 2 == j, lambda c, j: outward(c + HALO) == j],
        [lambda c, j: (c + HALO) // 2 == j],
        [lambda c, j: (c + HALO == 2 * j) & (c > 0)],
        [lambda x, j: (x < 32) & (x != 15) & (x != 16) & (column(x) // 2 == j)],
        [lambda x, j: (x < 32) & (column(x) == 2 * j)],
        [turn_test(0)],
        [turn_test(1)],
    ]
    + level_tests(0, LANES)
    + level_tests(1, 8)
    + [
        [lambda j, x: x // 2 == j],
        [lambda j, x: j == x // 2 + HALO // 2],
        [lambda x, j: x % 8 == j // HALO],
    ]
)


def pack_rows_kernel(res_ref, ground_ref, nodata_ref, patch_ref, first_ref, second_ref, real_ref, whole_ref, sem_ref):
    rows = res_ref.shape[0]
    starts = (0, rows - HALO)
    copies = []
    for which, source in enumerate((res_ref, ground_ref, nodata_ref, patch_ref)):
        near_ref = real_ref if which < 2 else whole_ref
        for end in range(2):
            target = near_ref.at[2 * (which % 2) + end]
            part = source.at[pl.ds(starts[end], HALO)]
            copies.append(pltpu.make_async_copy(part, target, sem_ref.at[2 * which + end]))
    for copy in copies:
        copy.start()
    for copy in copies:
        copy.wait()
    odd = lax.axis_index("row") % 2 == 1
    for which in range(4):
        if which < 2:
            top, bottom = real_ref[2 * which], real_ref[2 * which + 1]
        elif which == 2:
            top, bottom = (jnp.where(whole_ref[end] == 0, 1.0, 0.0) for end in range(2))
        else:
            top, bottom = whole_ref[2].astype(F32), whole_ref[3].astype(F32)
        part = pl.ds(which * HALO, HALO)
        first_ref[part] = jnp.where(odd, top, bottom)
        second_ref[part] = jnp.where(odd, bottom, top)


def prepare_kernel(res_ref, ground_ref, nodata_ref, patch_ref, order_ref, tall_ref, first_ref, second_ref, *rest):
    table_refs = rest[: len(TABLES)]
    nodata_near_ref, patch_near_ref, sem_ref = rest[len(TABLES) :]
    rows = res_ref.shape[0]
    middle = pl.ds(HALO, rows)
    copies = [
        pltpu.make_async_copy(source, target, sem_ref.at[which])
        for which, (source, target) in enumerate(
            (
                (res_ref, tall_ref.at[0, middle]),
                (ground_ref, tall_ref.at[1, middle]),
                (nodata_ref, nodata_near_ref),
                (patch_ref, patch_near_ref),
            )
        )
    ]
    for copy in copies:
        copy.start()
    for tests, table_ref in zip(TABLES, table_refs):
        table_ref[...] = stacked(jnp.concatenate([selection(LANES, test) for test in tests], axis=0))
    for copy in copies:
        copy.wait()
    tall_ref[2, middle] = jnp.where(nodata_near_ref[...] == 0, 1.0, 0.0)
    tall_ref[3, middle] = patch_near_ref[...].astype(F32)
    half = rows // 2
    shape = first_ref.shape
    group_of = iota(shape, 1) // HALO
    odd = lax.axis_index("col") % 2 == 1
    to_right = jnp.zeros(shape, F32)
    to_left = jnp.zeros(shape, F32)
    edge = jnp.zeros((HALO, shape[1]), F32)
    for which in range(4):
        upper = jnp.concatenate([edge, tall_ref[which, pl.ds(HALO, half)]], axis=0)
        lower = jnp.concatenate([tall_ref[which, pl.ds(HALO + half, half)], edge], axis=0)
        for side, values in enumerate((upper, lower)):
            group = 2 * which + side
            here = group_of == group
            to_right = jnp.where(here, rot(values, HALO * group + HALO, 1), to_right)
            to_left = jnp.where(here, rot(values, HALO * group, 1), to_left)
    first_ref[...] = jnp.where(odd, to_left, to_right)
    second_ref[...] = jnp.where(odd, to_right, to_left)


def before_after(axis, first, second):
    index = lax.axis_index(axis)
    odd = index % 2 == 1
    before = jnp.where(index > 0, jnp.where(odd, first, second), 0.0)
    after = jnp.where(index < lax.axis_size(axis) - 1, jnp.where(odd, second, first), 0.0)
    return before, after


def pack_cols_kernel(
    from_first_ref, from_second_ref, tall_in_ref, first_in_ref, second_in_ref, tall_ref, first_ref, second_ref
):
    rows = tall_ref.shape[1]
    ends = (pl.ds(0, HALO), pl.ds(rows // 2 - HALO, HALO))
    odd = lax.axis_index("col") % 2 == 1
    nearby = before_after("row", from_first_ref[...], from_second_ref[...])
    group_of = iota((HALO, LANES), 1) // HALO
    for side in range(2):
        first = first_in_ref[ends[side], :]
        second = second_in_ref[ends[side], :]
        for which in range(4):
            values = nearby[side][which * HALO : which * HALO + HALO]
            if which < 2:
                values = jnp.where(values > 0, values, 1.0)
            tall_ref[which, pl.ds(side * (rows - HALO), HALO)] = values
            group = 2 * which + side
            here = group_of == group
            to_right = rot(values, HALO * group + HALO, 1)
            to_left = rot(values, HALO * group, 1)
            first = jnp.where(here, jnp.where(odd, to_left, to_right), first)
            second = jnp.where(here, jnp.where(odd, to_right, to_left), second)
        first_ref[ends[side], :] = first
        second_ref[ends[side], :] = second


def link(resist, validity, near_resist, near_valid):
    return (validity * near_valid) * (2.0 / (resist + near_resist))


def weights_of(diag):
    return OMEGA / jnp.where(diag > 0, diag, 1.0)


def level_0(fields, odd_column, west, east):
    res, ground, val, patch = fields
    link_w = [west(res[i], val[i], i) for i in range(2)]
    link_e = [east(link_w[i], i) for i in range(2)]
    v_in = link(res[0], val[0], res[1], val[1])
    v_up = link(res[0], val[0], rot(res[1], 1, 0), rot(val[1], 1, 0))
    v_dn = rot(v_up, -1, 0)
    vertical = (v_up, v_dn)
    weight, own, side, away = [], [], [], []
    for i in range(2):
        w = weights_of(ground[i] + v_in + vertical[i] + link_w[i] + link_e[i])
        own.append((1.0 - OMEGA) * val[i] + w * (v_in + jnp.where(odd_column, link_w[i], link_e[i])))
        side.append(w * jnp.where(odd_column, link_e[i], link_w[i]))
        away.append(w * vertical[i])
        weight.append(w * val[i])
    away = [rot(away[0], -1, 0), rot(away[1], 1, 0)]
    return weight, own, side, away, link_w, v_up


def choices(patch, values):
    spread = jnp.where(patch > 0, -0.125, 0.0)
    return [(0.875 * value, spread * value) for value in values]


def pick(test, choice):
    return jnp.where(test, choice[0], choice[1])


def rows_by_parity(ref, which):
    half = ref.shape[1] // 2
    return [ref[which, pl.ds(start, half, stride=2), :] for start in range(2)]


def inner_kernel(tall_ref, both_ref, sum_ref, even_ref, r1_ref, c1_ref, w0_ref, edge_ref, west_ref):
    half = tall_ref.shape[1] // 2
    lane = iota((half, LANES), 1)
    fields = [rows_by_parity(tall_ref, which) for which in range(4)]
    patch = fields[3]
    odd = lane % 2 == 1
    weight, own, side, away, west, v_up = level_0(
        fields,
        odd,
        lambda res, val, i: link(res, val, rot(res, 1, 1), rot(val, 1, 1)),
        lambda value, i: rot(value, -1, 1),
    )
    inside = (lane > 0) & (lane < LANES - 1)
    own, side, away = ([jnp.where(inside, value, 0.0) for value in pair] for pair in (own, side, away))
    kept = slice(HALO // 2, half - HALO // 2)
    for i in range(2):
        w0_ref[i] = weight[i][kept]
        west_ref[i] = jnp.where(lane == 15, rot(west[i], 14, 1), rot(west[i], 17, 1))
    whole_lane = iota((2 * half, LANES), 1)
    for which in range(4):
        value = tall_ref[which]
        edge_ref[which] = jnp.where(whole_lane == 15, rot(value, 15, 1), rot(value, 17, 1))
    c1_ref[0] = dot01([fields[1][0] + fields[1][1]], sum_ref[...])
    c1_ref[1] = dot01([v_up], sum_ref[...])
    c1_ref[2] = dot01([west[0] + west[1]], even_ref[...])
    near = [choices(patch[i], (own[i], side[i])) for i in range(2)]
    patch_away = [rot(patch[0], -1, 0), rot(patch[1], 1, 0)]
    far = [choices(patch_away[i], (away[i],)) for i in range(2)]
    for k in range(RHS - 1):
        tests = [patch[i] == k + 1.0 for i in range(2)]
        tests_away = [patch_away[i] == k + 1.0 for i in range(2)]
        to_own = pick(tests[0], near[0][0]) + pick(tests[1], near[1][0])
        to_own = to_own + (pick(tests_away[0], far[0][0]) + pick(tests_away[1], far[1][0]))
        to_side = pick(tests[0], near[0][1]) + pick(tests[1], near[1][1])
        r1_ref[k] = dot01([to_own, to_side], both_ref[...])


def down_kernel(
    from_first_ref,
    from_second_ref,
    r1_inner_ref,
    c1_inner_ref,
    w0_inner_ref,
    edge_ref,
    west_ref,
    sum_ref,
    even_ref,
    turn_first_ref,
    turn_second_ref,
    usual_both_ref,
    usual_sum_ref,
    usual_even_ref,
    last_both_ref,
    last_sum_ref,
    last_even_ref,
    payload_ref,
    w0_ref,
    r1_ref,
    r2_ref,
    r3_ref,
    w1_ref,
    w2_ref,
    w3_ref,
    ext_ref,
    c1_ref,
    c2_ref,
    c3_ref,
):
    devices = payload_ref.shape[0]
    n1 = edge_ref.shape[1] // 2
    lane = iota((n1, LANES), 1)
    from_left, from_right = before_after("col", from_first_ref[...], from_second_ref[...])
    at_left = (lane < 15) | (lane == LANES - 1)
    at_edge = (lane == 15) | (lane == 16)
    at_right = (lane > 16) & (lane < 33)
    for which in range(4):
        for part in range(2):
            group = 2 * which + part
            rows = pl.ds(part * n1, n1)
            value = jnp.where(at_right, rot(from_right, 17 - HALO * group, 1), 0.0)
            value = jnp.where(at_left, rot(from_left, -1 - HALO * group, 1), value)
            value = jnp.where(at_edge, edge_ref[which, rows, :], value)
            if which < 2:
                value = jnp.where(value > 0, value, 1.0)
            ext_ref[which, rows, :] = value
    fields = [rows_by_parity(ext_ref, which) for which in range(4)]
    weight, own, side, away, west, v_up = level_0(
        fields,
        lane % 2 == 0,
        lambda res, val, i: jnp.where(
            lane == 16, west_ref[i], link(res, val, rot(res, 1, 1), rot(val, 1, 1))
        ),
        lambda value, i: jnp.where(lane == 15, west_ref[i], rot(value, -1, 1)),
    )
    kept = slice(HALO // 2, n1 - HALO // 2)
    for i in range(2):
        value = weight[i][kept]
        full = iota(value.shape, 1)
        w0_ref[i] = jnp.where(
            full == 0, value[:, 15:16], jnp.where(full == LANES - 1, value[:, 16:17], w0_inner_ref[i])
        )

    zeros = jnp.zeros((c1_ref.shape[1] - n1, LANES), F32)
    c1_ref[0, 0:n1] = c1_inner_ref[0] + dot01([fields[1][0] + fields[1][1]], sum_ref[...])
    c1_ref[1, 0:n1] = c1_inner_ref[1] + dot01([v_up], sum_ref[...])
    c1_ref[2, 0:n1] = c1_inner_ref[2] + dot01([west[0] + west[1]], even_ref[...])
    for index in range(3):
        c1_ref[index, n1:] = zeros

    outer = lane < 32

    def twice(value):
        return value + rot(value, 64, 1)

    own, side, away, patch = (
        [jnp.where(outer, value, 0.0) for value in pair] for pair in (own, side, away, fields[3])
    )
    patch = [value + rot(value, 32, 1) for value in patch]
    later = jnp.where(lane >= 64, 1.0, 0.0)
    patch = [twice(value) for value in patch]
    both = [twice(own[i] + rot(side[i], 32, 1)) for i in range(2)]
    away = [twice(value) for value in away]
    patch_away = [rot(patch[0], -1, 0), rot(patch[1], 1, 0)]
    terms = []
    for value, entry in ((patch[0], both[0]), (patch[1], both[1]), (patch_away[0], away[0]), (patch_away[1], away[1])):
        terms.append((value - later, choices(value, (entry,))[0]))

    turns = (turn_first_ref, turn_second_ref)
    for first in range(0, RHS, 2):
        picked = [pick(value == first + 1.0, choice) for value, choice in terms]
        outer_part = (picked[0] + picked[1]) + (picked[2] + picked[3])
        for k in range(first, min(first + 2, RHS - 1)):
            r1_ref[k, 0:n1] = r1_inner_ref[k] + dot01([outer_part], turns[k - first][...])
            r1_ref[k, n1:] = zeros

    usual = (usual_both_ref, usual_sum_ref, usual_even_ref)
    last = (last_both_ref, last_sum_ref, last_even_ref)
    for r_ref, c_ref, w_ref, next_r, next_c in (
        (r1_ref, c1_ref, w1_ref, r2_ref, c2_ref),
        (r2_ref, c2_ref, w2_ref, r3_ref, c3_ref),
        (r3_ref, c3_ref, w3_ref, None, None),
    ):
        half = r_ref.shape[1] // 2
        even, uneven = pl.ds(0, half, stride=2), pl.ds(1, half, stride=2)
        odd_lane = iota((half, LANES), 1) % 2 == 1
        ge, go = c_ref[0, even, :], c_ref[0, uneven, :]
        v_up, v_in = c_ref[1, even, :], c_ref[1, uneven, :]
        we, wo = c_ref[2, even, :], c_ref[2, uneven, :]
        ee, eo = rot(we, -1, 1), rot(wo, -1, 1)
        v_dn = rot(v_up, -1, 0)
        w_e = weights_of(ge + v_up + v_in + we + ee)
        w_o = weights_of(go + v_in + v_dn + wo + eo)
        a_e = (1.0 - OMEGA) + w_e * (v_in + jnp.where(odd_lane, we, ee))
        a_o = (1.0 - OMEGA) + w_o * (v_in + jnp.where(odd_lane, wo, eo))
        b_e = w_e * jnp.where(odd_lane, ee, we)
        b_o = w_o * jnp.where(odd_lane, eo, wo)
        c_e = w_e * v_up
        c_o = w_o * v_dn
        w_ref[0] = w_e
        w_ref[1] = w_o
        both, inner, evens = (table[...] for table in (usual if next_r is not None else last))
        coarser = [dot01([ge + go], inner), dot01([v_up], inner), dot01([we + wo], evens)]
        fields = []
        for k in range(RHS - 1):
            re, ro = r_ref[k, even, :], r_ref[k, uneven, :]
            own = a_e * re + a_o * ro + rot(c_o * ro, 1, 0) + rot(c_e * re, -1, 0)
            side = b_e * re + b_o * ro
            fields.append(dot01([own, side], both))
        if next_r is not None:
            for index in range(3):
                next_c[index] = coarser[index]
            for k in range(RHS - 1):
                next_r[k] = fields[k]

    shape = fields[0].shape
    mine = iota(shape, 1) // 8 == iota(shape, 0) - 1

    def flat(field):
        return jnp.sum(jnp.where(mine, field, 0.0), axis=0, keepdims=True)

    sub = iota((8, LANES), 0)
    lane8 = iota((8, LANES), 1)
    links = jnp.where(sub < 4, flat(coarser[1]), flat(coarser[2]))
    turned = rot(links, 96, 1)
    for row in (1, 2):
        turned = jnp.where(sub % 4 == row, rot(links, 96 - 32 * row, 1), turned)
    tile = jnp.broadcast_to(flat(coarser[0]), (8, LANES))
    for k in range(RHS - 1):
        tile = jnp.where(sub == k, flat(fields[k]), tile)
    tile = jnp.where(lane8 < 96, tile, turned)

    @pl.loop(0, devices)
    def _(device):
        payload_ref[device] = tile


def up_kernel(
    tall_ref,
    w0_ref,
    r1_ref,
    r2_ref,
    r3_ref,
    w1_ref,
    w2_ref,
    w3_ref,
    spread_ref,
    finest_ref,
    base_ref,
    t3_ref,
    t2_ref,
    t1_ref,
):
    for r_ref, w_ref, coarse_ref, t_ref in (
        (r3_ref, w3_ref, None, t3_ref),
        (r2_ref, w2_ref, t3_ref, t2_ref),
        (r1_ref, w1_ref, t2_ref, t1_ref),
    ):
        half = w_ref.shape[1]
        for k in range(RHS - 1):
            finer = None if coarse_ref is None else dot01([coarse_ref[k]], spread_ref[...])
            for index in range(2):
                rows = pl.ds(index, half, stride=2)
                smoothed = w_ref[index] * r_ref[k, rows, :]
                t_ref[k, rows, :] = smoothed if finer is None else finer + smoothed
    half = w0_ref.shape[1]
    sides = []
    for index in range(2):
        rows = pl.ds(index, half, stride=2)
        patch = tall_ref[3, pl.ds(HALO + index, half, stride=2), :]
        sides.append((rows, patch, choices(patch, (w0_ref[index],))[0]))
    left_over = None
    for k in range(RHS):
        if k + 1 < RHS:
            coarse = t1_ref[k, pl.ds(HALO // 2, half)]
            left_over = -coarse if left_over is None else left_over - coarse
        else:
            coarse = left_over
        finer = dot01([coarse], finest_ref[...])
        for rows, patch, choice in sides:
            base_ref[k, rows, :] = finer + pick(patch == k + 1.0, choice)


def solve_kernel(
    grid,
    all_ref,
    base_ref,
    widen_ref,
    out_ref,
    coef_ref,
    x_ref,
    r_ref,
    q_ref,
    p_ref,
    p_up_ref,
    p_down_ref,
    p_first_ref,
    p_last_ref,
    u_ref,
    done_ref,
    sem_ref,
):
    grid_rows, grid_cols = grid
    count = grid_rows * grid_cols
    lane = iota((8, LANES), 1)
    column = lane % 8

    def choose(test, yes, no):
        if isinstance(test, bool):
            return yes if test else no
        return jnp.where(test, yes, no)

    def at(t):
        return pl.ds(8 * t if isinstance(t, int) else pl.multiple_of(8 * t, 8), 8)

    def every(body, init):
        if count <= 64:
            for tile in range(count):
                init = body(tile, init)
            return init
        return lax.fori_loop(0, count, body, init)

    all_lane = iota((count, LANES), 1)
    inside = all_lane < 96
    rows = [all_ref[pl.ds(i, count, stride=8), :] for i in range(8)]
    north, west = (
        jnp.where(
            all_lane < 32,
            rot(rows[i], 32, 1),
            jnp.where(all_lane < 64, rot(rows[i + 1], 64, 1), rot(rows[i + 2], 96, 1)),
        )
        for i in (0, 4)
    )
    north, west = jnp.where(inside, north, 0.0), jnp.where(inside, west, 0.0)
    north_below = jnp.concatenate([north[grid_cols:], jnp.zeros((grid_cols, LANES), F32)], axis=0)
    south = jnp.where(all_lane >= 88, rot(north_below, 88, 1), rot(north, 120, 1))
    west_right = jnp.where(iota((count, LANES), 0) % grid_cols < grid_cols - 1, rot(west, -1, 0), 0.0)
    east = jnp.where(all_lane % 8 == 7, rot(west_right, 7, 1), rot(west, 127, 1))
    south, east = jnp.where(inside, south, 0.0), jnp.where(inside, east, 0.0)
    coef_ref[0] = jnp.where(inside, rows[7], 0.0) + north + south + west + east
    coef_ref[1] = north
    coef_ref[2] = south
    coef_ref[3] = west
    coef_ref[4] = east
    others = ((rows[0] + rows[1]) + (rows[2] + rows[3])) + ((rows[4] + rows[5]) + rows[6])
    r_ref[...] = jnp.where(iota(r_ref.shape, 1) < 96, all_ref[...], 0.0)
    r_ref[pl.ds(7, count, stride=8), :] = jnp.where(inside, -others, 0.0)

    def total(values):
        return jnp.sum(values, axis=1, keepdims=True)

    def direct(t, values):
        p_ref[at(t), :] = values
        p_up_ref[at(t), :] = rot(values, 8, 1)
        p_down_ref[at(t), :] = rot(values, 120, 1)
        p_last_ref[at(t), :] = rot(values, 40, 1)
        p_first_ref[at(t), :] = rot(values, 88, 1)

    def begin(t, norm):
        values = r_ref[at(t), :]
        direct(t, values)
        return norm + values * values

    zero = jnp.zeros((8, LANES), F32)
    rr = total(every(begin, zero))

    def coef_of(index, t):
        return coef_ref[index, pl.ds(t, 8, stride=0), :]

    def image_of(t, dot):
        here = p_ref[at(t), :]
        up = p_last_ref[at(choose(t >= grid_cols, t - grid_cols, t)), :]
        down = p_first_ref[at(choose(t + grid_cols < count, t + grid_cols, t)), :]
        left = p_down_ref[at(choose(t % grid_cols > 0, t - 1, t)), :]
        right = p_up_ref[at(choose(t % grid_cols < grid_cols - 1, t + 1, t)), :]
        up = jnp.where(lane < 8, up, p_up_ref[at(t), :])
        down = jnp.where(lane >= 88, down, p_down_ref[at(t), :])
        left = rot(jnp.where(column == 7, left, here), 1, 1)
        right = rot(jnp.where(column == 0, right, here), -1, 1)
        pulled = coef_of(1, t) * up + coef_of(2, t) * down
        pulled = pulled + coef_of(3, t) * left + coef_of(4, t) * right
        image = coef_of(0, t) * here - pulled
        q_ref[at(t), :] = image
        return dot + here * image

    for sweep in range(ITERS - 1):
        step = jnp.broadcast_to(rr / total(every(image_of, zero)), (8, LANES))

        def advance(t, norm):
            left_over = r_ref[at(t), :] - step * q_ref[at(t), :]
            r_ref[at(t), :] = left_over
            return norm + left_over * left_over

        new = total(every(advance, zero))
        ratio = jnp.broadcast_to(new / rr, (8, LANES))
        rr = new

        def turn(t, carry):
            values = p_ref[at(t), :]
            gain = step * values
            x_ref[at(t), :] = gain if sweep == 0 else x_ref[at(t), :] + gain
            direct(t, r_ref[at(t), :] + ratio * values)
            return carry

        every(turn, 0)

    step = jnp.broadcast_to(rr / total(every(image_of, zero)), (8, LANES))
    device = lax.axis_index("row") * grid_cols + lax.axis_index("col")
    mine = x_ref[at(device), :] + step * p_ref[at(device), :]
    groups = u_ref.shape[0] // 8
    placed = jnp.concatenate([jnp.where(lane // 8 == i, mine, 0.0) for i in range(groups)], axis=0)
    u_ref[...] = dot01([placed], widen_ref[...])
    copies = []
    for k in range(RHS):
        for i in range(groups):
            coarse = u_ref[pl.ds(8 * i + k, 8, stride=0), :]
            for part in range(HALO // 8):
                rows = pl.ds(HALO * i + 8 * part, 8)
                done_ref[k, rows, :] = base_ref[k, rows, :] + coarse
        copy = pltpu.make_async_copy(done_ref.at[k], out_ref.at[k], sem_ref.at[k])
        copy.start()
        copies.append(copy)
    for copy in copies:
        copy.wait()


def exchanged(first, second, axis, other):
    sizes = {name: lax.axis_size(name) for name in (axis, other)}

    def pairs(step):
        found = []
        for i in range(sizes["row"]):
            for j in range(sizes["col"]):
                place = {"row": i, "col": j}
                target = dict(place)
                at = place[axis]
                if step == 0:
                    target[axis] = at ^ 1
                elif at in (0, sizes[axis] - 1):
                    target[other] = place[other] ^ 1
                else:
                    target[axis] = at + 1 if at % 2 else at - 1
                found.append((i * sizes["col"] + j, target["row"] * sizes["col"] + target["col"]))
        return found

    return [lax.ppermute(part, ("row", "col"), pairs(step)) for step, part in enumerate((first, second))]


def shards(resistance, ground, nodata, patch_ids):
    grid = (lax.axis_size("row"), lax.axis_size("col"))
    devices = grid[0] * grid[1]
    rows, cols = resistance.shape
    own = [pltpu.with_memory_space_constraint(part, pltpu.HBM) for part in (resistance, ground, nodata, patch_ids)]
    def near(value):
        return pltpu.with_memory_space_constraint(value, pltpu.VMEM)

    def call(kernel, outs, scratch, *args, **options):
        outs = tuple(pltpu.VMEM(out, F32) if isinstance(out, tuple) else out for out in outs)
        scratch = [pltpu.VMEM(part, F32) if isinstance(part, tuple) else part for part in scratch]
        name = kernel.__name__
        params = pltpu.CompilerParams(vmem_limit_bytes=VMEM_LIMIT)
        return pl.pallas_call(
            kernel, out_shape=outs, scratch_shapes=scratch, name=name, compiler_params=params, **options
        )(*args)

    def all_near(values):
        return [near(value) for value in values]

    strip = (4 * HALO, cols)
    hbm = [pl.BlockSpec(memory_space=pltpu.HBM)] * 4
    near_whole = pltpu.VMEM((4, HALO, cols), jnp.int32)
    first, second = call(
        pack_rows_kernel,
        [strip, strip],
        [(4, HALO, cols), near_whole, pltpu.SemaphoreType.DMA((8,))],
        *own,
        in_specs=hbm,
    )
    tall_rows = rows + 2 * HALO
    n1 = tall_rows // 2
    tall, first_cols, second_cols, *tables = all_near(
        call(
            prepare_kernel,
            [(4, tall_rows, cols), (n1, LANES), (n1, LANES)]
            + [pltpu.VMEM((PIECES * LANES * len(tests), LANES), BF16) for tests in TABLES],
            [pltpu.VMEM((rows, cols), jnp.int32)] * 2 + [pltpu.SemaphoreType.DMA((4,))],
            *own,
            near(first),
            in_specs=hbm + [pl.BlockSpec(memory_space=pltpu.VMEM)],
            cost_estimate=pl.CostEstimate(flops=10**8, bytes_accessed=10**6, transcendentals=0),
        )
    )
    first, second = exchanged(first, second, "row", "col")
    tall, first, second = call(
        pack_cols_kernel,
        [(4, tall_rows, cols), (n1, LANES), (n1, LANES)],
        [],
        near(first),
        near(second),
        tall,
        first_cols,
        second_cols,
        input_output_aliases={2: 0, 3: 1, 4: 2},
    )
    tall = near(tall)
    first, second = exchanged(first, second, "col", "row")
    sizes = [128, 64, 32]
    inner = call(
        inner_kernel,
        [(RHS - 1, n1, LANES), (3, n1, LANES), (2, rows // 2, LANES), (4, tall_rows, LANES), (2, n1, LANES)],
        [],
        tall,
        *tables[:3],
        cost_estimate=pl.CostEstimate(flops=10**8, bytes_accessed=10**6, transcendentals=0),
    )
    payload, w0, *levels = call(
        down_kernel,
        [(devices, 8, LANES), (2, rows // 2, LANES)]
        + [(RHS - 1, size, LANES) for size in sizes]
        + [(2, size // 2, LANES) for size in sizes],
        [(4, tall_rows, LANES)] + [(3, size, LANES) for size in sizes],
        *all_near((first, second, *inner)),
        *tables[3:13],
    )
    everything = lax.all_to_all(payload, ("row", "col"), 0, 0)
    (base,) = call(
        up_kernel,
        [(RHS, rows, cols)],
        [(RHS - 1, size, LANES) for size in sizes[::-1]],
        tall,
        *all_near([w0] + levels),
        *tables[13:15],
        cost_estimate=pl.CostEstimate(flops=10**8, bytes_accessed=10**6, transcendentals=0),
    )
    return pl.pallas_call(
        functools.partial(solve_kernel, grid),
        out_shape=jax.ShapeDtypeStruct((RHS, rows, cols), F32),
        out_specs=pl.BlockSpec(memory_space=pl.ANY),
        scratch_shapes=[pltpu.VMEM((5, devices, LANES), F32)]
        + [pltpu.VMEM((devices * 8, LANES), F32)] * 8
        + [pltpu.VMEM((rows // HALO * 8, LANES), F32), pltpu.VMEM((RHS, rows, cols), F32)]
        + [pltpu.SemaphoreType.DMA((RHS,))],
        compiler_params=pltpu.CompilerParams(vmem_limit_bytes=VMEM_LIMIT),
        name="solve_kernel",
    )(near(everything.reshape(devices * 8, LANES)), near(base), tables[15])


def solution(mesh):
    spec = P("row", "col")
    return jax.shard_map(shards, mesh=mesh, in_specs=(spec,) * 4, out_specs=P(None, "row", "col"), check_vma=False)
```

```python
import functools

import jax
import jax.numpy as jnp
from jax import lax
from jax.experimental import pallas as pl
from jax.experimental.pallas import tpu as pltpu
from jax.sharding import PartitionSpec as P

RHS = 8
ITERS = 4
OMEGA = 0.8
HALO = 16
LANES = 128
F32 = jnp.float32
BF16 = jnp.bfloat16
PIECES = 2
VMEM_LIMIT = 32 * 2**20


def iota(shape, dim):
    return lax.broadcasted_iota(jnp.int32, shape, dim)


def selection(rows, test):
    shape = (rows, LANES)
    return jnp.where(test(iota(shape, 0), iota(shape, 1)), 1.0, 0.0).astype(BF16)


def split(values):
    pieces = []
    for piece in range(PIECES):
        pieces.append(values.astype(BF16))
        if piece + 1 < PIECES:
            values = values - pieces[-1].astype(F32)
    return pieces


def stacked(matrix):
    return jnp.concatenate([matrix] * PIECES, axis=0)


def dot01(parts, matrix):
    pieces = [split(part) for part in parts]
    rows = jnp.concatenate([piece[i] for i in range(PIECES) for piece in pieces], axis=1)
    return jnp.dot(rows, matrix, preferred_element_type=F32)


def rot(values, shift, axis):
    return pltpu.roll(values, shift % values.shape[axis], axis)


def column(x):
    return jnp.where(x < 16, x + 1, x + 127)


def outward(x):
    return x // 2 + 2 * (x % 2) - 1


def turn_test(first):
    def test(x, j):
        y = x - 64 * first
        own = (y >= 0) & (y < 32) & (column(y) // 2 == j)
        return own | ((y >= 32) & (y < 64) & (outward(column(y - 32)) == j))

    return test


def level_tests(shift, places):
    m_in = lambda x, j: x // 2 - shift == j % places
    m_out = lambda x, j: outward(x) - shift == j % places
    m_even = lambda x, j: (x // 2 - shift == j % places) & (x % 2 == 0)
    return [[m_in, m_out], [m_in], [m_even]]


TABLES = (
    [
        [lambda c, j: (c + HALO) // 2 == j, lambda c, j: outward(c + HALO) == j],
        [lambda c, j: (c + HALO) // 2 == j],
        [lambda c, j: (c + HALO == 2 * j) & (c > 0)],
        [lambda x, j: (x < 32) & (x != 15) & (x != 16) & (column(x) // 2 == j)],
        [lambda x, j: (x < 32) & (column(x) == 2 * j)],
        [turn_test(0)],
        [turn_test(1)],
    ]
    + level_tests(0, LANES)
    + level_tests(1, 8)
    + [
        [lambda j, x: x // 2 == j],
        [lambda j, x: j == x // 2 + HALO // 2],
        [lambda x, j: x % 8 == j // HALO],
    ]
)


def pack_rows_kernel(res_ref, ground_ref, nodata_ref, patch_ref, first_ref, second_ref, real_ref, whole_ref, sem_ref):
    rows = res_ref.shape[0]
    starts = (0, rows - HALO)
    copies = []
    for which, source in enumerate((res_ref, ground_ref, nodata_ref, patch_ref)):
        near_ref = real_ref if which < 2 else whole_ref
        for end in range(2):
            target = near_ref.at[2 * (which % 2) + end]
            part = source.at[pl.ds(starts[end], HALO)]
            copies.append(pltpu.make_async_copy(part, target, sem_ref.at[2 * which + end]))
    for copy in copies:
        copy.start()
    for copy in copies:
        copy.wait()
    odd = lax.axis_index("row") % 2 == 1
    for which in range(4):
        if which < 2:
            top, bottom = real_ref[2 * which], real_ref[2 * which + 1]
        elif which == 2:
            top, bottom = (jnp.where(whole_ref[end] == 0, 1.0, 0.0) for end in range(2))
        else:
            top, bottom = whole_ref[2].astype(F32), whole_ref[3].astype(F32)
        part = pl.ds(which * HALO, HALO)
        first_ref[part] = jnp.where(odd, top, bottom)
        second_ref[part] = jnp.where(odd, bottom, top)


def prepare_kernel(res_ref, ground_ref, nodata_ref, patch_ref, order_ref, tall_ref, first_ref, second_ref, *rest):
    table_refs = rest[: len(TABLES)]
    nodata_near_ref, patch_near_ref, sem_ref = rest[len(TABLES) :]
    rows = res_ref.shape[0]
    middle = pl.ds(HALO, rows)
    copies = [
        pltpu.make_async_copy(source, target, sem_ref.at[which])
        for which, (source, target) in enumerate(
            (
                (res_ref, tall_ref.at[0, middle]),
                (ground_ref, tall_ref.at[1, middle]),
                (nodata_ref, nodata_near_ref),
                (patch_ref, patch_near_ref),
            )
        )
    ]
    for copy in copies:
        copy.start()
    for tests, table_ref in zip(TABLES, table_refs):
        table_ref[...] = stacked(jnp.concatenate([selection(LANES, test) for test in tests], axis=0))
    for copy in copies:
        copy.wait()
    tall_ref[2, middle] = jnp.where(nodata_near_ref[...] == 0, 1.0, 0.0)
    tall_ref[3, middle] = patch_near_ref[...].astype(F32)
    half = rows // 2
    shape = first_ref.shape
    group_of = iota(shape, 1) // HALO
    odd = lax.axis_index("col") % 2 == 1
    to_right = jnp.zeros(shape, F32)
    to_left = jnp.zeros(shape, F32)
    edge = jnp.zeros((HALO, shape[1]), F32)
    for which in range(4):
        upper = jnp.concatenate([edge, tall_ref[which, pl.ds(HALO, half)]], axis=0)
        lower = jnp.concatenate([tall_ref[which, pl.ds(HALO + half, half)], edge], axis=0)
        for side, values in enumerate((upper, lower)):
            group = 2 * which + side
            here = group_of == group
            to_right = jnp.where(here, rot(values, HALO * group + HALO, 1), to_right)
            to_left = jnp.where(here, rot(values, HALO * group, 1), to_left)
    first_ref[...] = jnp.where(odd, to_left, to_right)
    second_ref[...] = jnp.where(odd, to_right, to_left)


def before_after(axis, first, second):
    index = lax.axis_index(axis)
    odd = index % 2 == 1
    before = jnp.where(index > 0, jnp.where(odd, first, second), 0.0)
    after = jnp.where(index < lax.axis_size(axis) - 1, jnp.where(odd, second, first), 0.0)
    return before, after


def pack_cols_kernel(
    from_first_ref, from_second_ref, tall_in_ref, first_in_ref, second_in_ref, tall_ref, first_ref, second_ref
):
    rows = tall_ref.shape[1]
    ends = (pl.ds(0, HALO), pl.ds(rows // 2 - HALO, HALO))
    odd = lax.axis_index("col") % 2 == 1
    nearby = before_after("row", from_first_ref[...], from_second_ref[...])
    group_of = iota((HALO, LANES), 1) // HALO
    for side in range(2):
        first = first_in_ref[ends[side], :]
        second = second_in_ref[ends[side], :]
        for which in range(4):
            values = nearby[side][which * HALO : which * HALO + HALO]
            if which < 2:
                values = jnp.where(values > 0, values, 1.0)
            tall_ref[which, pl.ds(side * (rows - HALO), HALO)] = values
            group = 2 * which + side
            here = group_of == group
            to_right = rot(values, HALO * group + HALO, 1)
            to_left = rot(values, HALO * group, 1)
            first = jnp.where(here, jnp.where(odd, to_left, to_right), first)
            second = jnp.where(here, jnp.where(odd, to_right, to_left), second)
        first_ref[ends[side], :] = first
        second_ref[ends[side], :] = second


def link(resist, validity, near_resist, near_valid):
    return (validity * near_valid) * (2.0 / (resist + near_resist))


def weights_of(diag):
    return OMEGA / jnp.where(diag > 0, diag, 1.0)


def level_0(fields, odd_column, west, east):
    res, ground, val, patch = fields
    link_w = [west(res[i], val[i], i) for i in range(2)]
    link_e = [east(link_w[i], i) for i in range(2)]
    v_in = link(res[0], val[0], res[1], val[1])
    v_up = link(res[0], val[0], rot(res[1], 1, 0), rot(val[1], 1, 0))
    v_dn = rot(v_up, -1, 0)
    vertical = (v_up, v_dn)
    weight, own, side, away = [], [], [], []
    for i in range(2):
        w = weights_of(ground[i] + v_in + vertical[i] + link_w[i] + link_e[i])
        own.append((1.0 - OMEGA) * val[i] + w * (v_in + jnp.where(odd_column, link_w[i], link_e[i])))
        side.append(w * jnp.where(odd_column, link_e[i], link_w[i]))
        away.append(w * vertical[i])
        weight.append(w * val[i])
    away = [rot(away[0], -1, 0), rot(away[1], 1, 0)]
    return weight, own, side, away, link_w, v_up


def choices(patch, values):
    spread = jnp.where(patch > 0, -0.125, 0.0)
    return [(0.875 * value, spread * value) for value in values]


def pick(test, choice):
    return jnp.where(test, choice[0], choice[1])


def rows_by_parity(ref, which):
    half = ref.shape[1] // 2
    return [ref[which, pl.ds(start, half, stride=2), :] for start in range(2)]


def inner_kernel(tall_ref, both_ref, sum_ref, even_ref, r1_ref, c1_ref, w0_ref, edge_ref, west_ref):
    half = tall_ref.shape[1] // 2
    lane = iota((half, LANES), 1)
    fields = [rows_by_parity(tall_ref, which) for which in range(4)]
    patch = fields[3]
    odd = lane % 2 == 1
    weight, own, side, away, west, v_up = level_0(
        fields,
        odd,
        lambda res, val, i: link(res, val, rot(res, 1, 1), rot(val, 1, 1)),
        lambda value, i: rot(value, -1, 1),
    )
    inside = (lane > 0) & (lane < LANES - 1)
    own, side, away = ([jnp.where(inside, value, 0.0) for value in pair] for pair in (own, side, away))
    kept = slice(HALO // 2, half - HALO // 2)
    for i in range(2):
        w0_ref[i] = weight[i][kept]
        west_ref[i] = jnp.where(lane == 15, rot(west[i], 14, 1), rot(west[i], 17, 1))
    whole_lane = iota((2 * half, LANES), 1)
    for which in range(4):
        value = tall_ref[which]
        edge_ref[which] = jnp.where(whole_lane == 15, rot(value, 15, 1), rot(value, 17, 1))
    c1_ref[0] = dot01([fields[1][0] + fields[1][1]], sum_ref[...])
    c1_ref[1] = dot01([v_up], sum_ref[...])
    c1_ref[2] = dot01([west[0] + west[1]], even_ref[...])
    near = [choices(patch[i], (own[i], side[i])) for i in range(2)]
    patch_away = [rot(patch[0], -1, 0), rot(patch[1], 1, 0)]
    far = [choices(patch_away[i], (away[i],)) for i in range(2)]
    for k in range(RHS - 1):
        tests = [patch[i] == k + 1.0 for i in range(2)]
        tests_away = [patch_away[i] == k + 1.0 for i in range(2)]
        to_own = pick(tests[0], near[0][0]) + pick(tests[1], near[1][0])
        to_own = to_own + (pick(tests_away[0], far[0][0]) + pick(tests_away[1], far[1][0]))
        to_side = pick(tests[0], near[0][1]) + pick(tests[1], near[1][1])
        r1_ref[k] = dot01([to_own, to_side], both_ref[...])


def down_kernel(
    from_first_ref,
    from_second_ref,
    r1_inner_ref,
    c1_inner_ref,
    w0_inner_ref,
    edge_ref,
    west_ref,
    sum_ref,
    even_ref,
    turn_first_ref,
    turn_second_ref,
    usual_both_ref,
    usual_sum_ref,
    usual_even_ref,
    last_both_ref,
    last_sum_ref,
    last_even_ref,
    payload_ref,
    w0_ref,
    r1_ref,
    r2_ref,
    r3_ref,
    w1_ref,
    w2_ref,
    w3_ref,
    ext_ref,
    c1_ref,
    c2_ref,
    c3_ref,
):
    n1 = edge_ref.shape[1] // 2
    lane = iota((n1, LANES), 1)
    from_left, from_right = before_after("col", from_first_ref[...], from_second_ref[...])
    from_right = rot(from_right, 18, 1)
    at_edge = (lane == 15) | (lane == 16)
    at_halo = (lane < 33) | (lane == LANES - 1)
    for which in range(4):
        for part in range(2):
            group = 2 * which + part
            rows = pl.ds(part * n1, n1)
            offset = (lane - HALO * group) % LANES
            value = jnp.where(offset < HALO, from_left, from_right)
            value = jnp.where(at_halo, rot(value, -1 - HALO * group, 1), 0.0)
            value = jnp.where(at_edge, edge_ref[which, rows, :], value)
            if which < 2:
                value = jnp.where(value > 0, value, 1.0)
            ext_ref[which, rows, :] = value
    fields = [rows_by_parity(ext_ref, which) for which in range(4)]
    weight, own, side, away, west, v_up = level_0(
        fields,
        lane % 2 == 0,
        lambda res, val, i: jnp.where(
            lane == 16, west_ref[i], link(res, val, rot(res, 1, 1), rot(val, 1, 1))
        ),
        lambda value, i: jnp.where(lane == 15, west_ref[i], rot(value, -1, 1)),
    )
    kept = slice(HALO // 2, n1 - HALO // 2)
    for i in range(2):
        value = weight[i][kept]
        full = iota(value.shape, 1)
        w0_ref[i] = jnp.where(
            full == 0, value[:, 15:16], jnp.where(full == LANES - 1, value[:, 16:17], w0_inner_ref[i])
        )

    zeros = jnp.zeros((c1_ref.shape[1] - n1, LANES), F32)
    c1_ref[0, 0:n1] = c1_inner_ref[0] + dot01([fields[1][0] + fields[1][1]], sum_ref[...])
    c1_ref[1, 0:n1] = c1_inner_ref[1] + dot01([v_up], sum_ref[...])
    c1_ref[2, 0:n1] = c1_inner_ref[2] + dot01([west[0] + west[1]], even_ref[...])
    for index in range(3):
        c1_ref[index, n1:] = zeros

    outer = lane < 32

    def twice(value):
        return value + rot(value, 64, 1)

    own, side, away, patch = (
        [jnp.where(outer, value, 0.0) for value in pair] for pair in (own, side, away, fields[3])
    )
    patch = [value + rot(value, 32, 1) for value in patch]
    later = jnp.where(lane >= 64, 1.0, 0.0)
    patch = [twice(value) for value in patch]
    both = [twice(own[i] + rot(side[i], 32, 1)) for i in range(2)]
    away = [twice(value) for value in away]
    patch_away = [rot(patch[0], -1, 0), rot(patch[1], 1, 0)]
    terms = []
    for value, entry in ((patch[0], both[0]), (patch[1], both[1]), (patch_away[0], away[0]), (patch_away[1], away[1])):
        terms.append((value - later, choices(value, (entry,))[0]))

    turns = (turn_first_ref, turn_second_ref)
    for first in range(0, RHS, 2):
        picked = [pick(value == first + 1.0, choice) for value, choice in terms]
        outer_part = (picked[0] + picked[1]) + (picked[2] + picked[3])
        for k in range(first, min(first + 2, RHS - 1)):
            r1_ref[k, 0:n1] = r1_inner_ref[k] + dot01([outer_part], turns[k - first][...])
            r1_ref[k, n1:] = zeros

    usual = (usual_both_ref, usual_sum_ref, usual_even_ref)
    last = (last_both_ref, last_sum_ref, last_even_ref)
    for r_ref, c_ref, w_ref, next_r, next_c in (
        (r1_ref, c1_ref, w1_ref, r2_ref, c2_ref),
        (r2_ref, c2_ref, w2_ref, r3_ref, c3_ref),
        (r3_ref, c3_ref, w3_ref, None, None),
    ):
        half = r_ref.shape[1] // 2
        even, uneven = pl.ds(0, half, stride=2), pl.ds(1, half, stride=2)
        odd_lane = iota((half, LANES), 1) % 2 == 1
        ge, go = c_ref[0, even, :], c_ref[0, uneven, :]
        v_up, v_in = c_ref[1, even, :], c_ref[1, uneven, :]
        we, wo = c_ref[2, even, :], c_ref[2, uneven, :]
        ee, eo = rot(we, -1, 1), rot(wo, -1, 1)
        v_dn = rot(v_up, -1, 0)
        w_e = weights_of(ge + v_up + v_in + we + ee)
        w_o = weights_of(go + v_in + v_dn + wo + eo)
        a_e = (1.0 - OMEGA) + w_e * (v_in + jnp.where(odd_lane, we, ee))
        a_o = (1.0 - OMEGA) + w_o * (v_in + jnp.where(odd_lane, wo, eo))
        b_e = w_e * jnp.where(odd_lane, ee, we)
        b_o = w_o * jnp.where(odd_lane, eo, wo)
        c_e = w_e * v_up
        c_o = w_o * v_dn
        w_ref[0] = w_e
        w_ref[1] = w_o
        both, inner, evens = (table[...] for table in (usual if next_r is not None else last))
        coarser = [dot01([ge + go], inner), dot01([v_up], inner), dot01([we + wo], evens)]
        fields = []
        for k in range(RHS - 1):
            re, ro = r_ref[k, even, :], r_ref[k, uneven, :]
            own = a_e * re + a_o * ro + rot(c_o * ro, 1, 0) + rot(c_e * re, -1, 0)
            side = b_e * re + b_o * ro
            fields.append(dot01([own, side], both))
        if next_r is not None:
            for index in range(3):
                next_c[index] = coarser[index]
            for k in range(RHS - 1):
                next_r[k] = fields[k]

    shape = fields[0].shape
    mine = iota(shape, 1) // 8 == iota(shape, 0) - 1

    def flat(field):
        return jnp.sum(jnp.where(mine, field, 0.0), axis=0, keepdims=True)

    sub = iota((8, LANES), 0)
    lane8 = iota((8, LANES), 1)
    links = jnp.where(sub < 4, flat(coarser[1]), flat(coarser[2]))
    turned = rot(links, 96, 1)
    for row in (1, 2):
        turned = jnp.where(sub % 4 == row, rot(links, 96 - 32 * row, 1), turned)
    tile = jnp.broadcast_to(flat(coarser[0]), (8, LANES))
    for k in range(RHS - 1):
        tile = jnp.where(sub == k, flat(fields[k]), tile)
    tile = jnp.where(lane8 < 96, tile, turned)

    payload_ref[...] = jnp.broadcast_to(tile, payload_ref.shape)


def up_kernel(
    tall_ref,
    w0_ref,
    r1_ref,
    r2_ref,
    r3_ref,
    w1_ref,
    w2_ref,
    w3_ref,
    spread_ref,
    finest_ref,
    base_ref,
    t3_ref,
    t2_ref,
    t1_ref,
):
    for r_ref, w_ref, coarse_ref, t_ref in (
        (r3_ref, w3_ref, None, t3_ref),
        (r2_ref, w2_ref, t3_ref, t2_ref),
        (r1_ref, w1_ref, t2_ref, t1_ref),
    ):
        half = w_ref.shape[1]
        for k in range(RHS - 1):
            finer = None if coarse_ref is None else dot01([coarse_ref[k]], spread_ref[...])
            for index in range(2):
                rows = pl.ds(index, half, stride=2)
                smoothed = w_ref[index] * r_ref[k, rows, :]
                t_ref[k, rows, :] = smoothed if finer is None else finer + smoothed
    half = w0_ref.shape[1]
    sides = []
    for index in range(2):
        rows = pl.ds(index, half, stride=2)
        patch = tall_ref[3, pl.ds(HALO + index, half, stride=2), :]
        sides.append((rows, patch, choices(patch, (w0_ref[index],))[0]))
    left_over = None
    for k in range(RHS):
        if k + 1 < RHS:
            coarse = t1_ref[k, pl.ds(HALO // 2, half)]
            left_over = -coarse if left_over is None else left_over - coarse
        else:
            coarse = left_over
        finer = dot01([coarse], finest_ref[...])
        for rows, patch, choice in sides:
            base_ref[k, rows, :] = finer + pick(patch == k + 1.0, choice)


def solve_kernel(
    grid,
    all_ref,
    base_ref,
    widen_ref,
    out_ref,
    coef_ref,
    x_ref,
    r_ref,
    q_ref,
    p_ref,
    p_up_ref,
    p_down_ref,
    u_ref,
    done_ref,
    sem_ref,
):
    grid_rows, grid_cols = grid
    count = grid_rows * grid_cols
    lane = iota((8, LANES), 1)
    column = lane % 8

    def choose(test, yes, no):
        if isinstance(test, bool):
            return yes if test else no
        return jnp.where(test, yes, no)

    def at(t):
        return pl.ds(8 * t if isinstance(t, int) else pl.multiple_of(8 * t, 8), 8)

    def every(body, init):
        if count <= 64:
            for tile in range(count):
                init = body(tile, init)
            return init
        return lax.fori_loop(0, count, body, init)

    all_lane = iota((count, LANES), 1)
    inside = all_lane < 96
    rows = [all_ref[pl.ds(i, count, stride=8), :] for i in range(8)]
    north, west = (
        jnp.where(
            all_lane < 32,
            rot(rows[i], 32, 1),
            jnp.where(all_lane < 64, rot(rows[i + 1], 64, 1), rot(rows[i + 2], 96, 1)),
        )
        for i in (0, 4)
    )
    north, west = jnp.where(inside, north, 0.0), jnp.where(inside, west, 0.0)
    north_below = jnp.concatenate([north[grid_cols:], jnp.zeros((grid_cols, LANES), F32)], axis=0)
    south = jnp.where(all_lane >= 88, rot(north_below, 88, 1), rot(north, 120, 1))
    west_right = jnp.where(iota((count, LANES), 0) % grid_cols < grid_cols - 1, rot(west, -1, 0), 0.0)
    east = jnp.where(all_lane % 8 == 7, rot(west_right, 7, 1), rot(west, 127, 1))
    south, east = jnp.where(inside, south, 0.0), jnp.where(inside, east, 0.0)
    diagonal = jnp.where(inside, rows[7], 0.0) + north + south + west + east
    for index, value in enumerate((diagonal, north, south, west, east)):
        for row in range(grid_rows):
            part = slice(row * grid_cols, (row + 1) * grid_cols)
            coef_ref[index, part] = rot(value[part], 96 * row, 1)
    others = ((rows[0] + rows[1]) + (rows[2] + rows[3])) + ((rows[4] + rows[5]) + rows[6])
    r_ref[...] = jnp.where(iota(r_ref.shape, 1) < 96, all_ref[...], 0.0)
    r_ref[pl.ds(7, count, stride=8), :] = jnp.where(inside, -others, 0.0)

    def total(values):
        return jnp.sum(values, axis=1, keepdims=True)

    def direct(t, values):
        p_ref[at(t), :] = values
        p_up_ref[at(t), :] = rot(values, 8, 1)
        p_down_ref[at(t), :] = rot(values, 120, 1)

    def begin(t, norm):
        values = pltpu.roll(r_ref[at(t), :], 96 * (t // grid_cols) % LANES, 1)
        r_ref[at(t), :] = values
        direct(t, values)
        return norm + values * values

    zero = jnp.zeros((8, LANES), F32)
    rr = total(every(begin, zero))

    def coef_of(index, t):
        return coef_ref[index, pl.ds(t, 8, stride=0), :]

    def image_of(t, dot):
        here = p_ref[at(t), :]
        up = p_up_ref[at(choose(t >= grid_cols, t - grid_cols, t)), :]
        down = p_down_ref[at(choose(t + grid_cols < count, t + grid_cols, t)), :]
        left = p_down_ref[at(choose(t % grid_cols > 0, t - 1, t)), :]
        right = p_up_ref[at(choose(t % grid_cols < grid_cols - 1, t + 1, t)), :]
        start = 12 * (t // grid_cols)
        up = jnp.where(lane // 8 == start % 16, up, p_up_ref[at(t), :])
        down = jnp.where(lane // 8 == (start + 11) % 16, down, p_down_ref[at(t), :])
        left = rot(jnp.where(column == 7, left, here), 1, 1)
        right = rot(jnp.where(column == 0, right, here), -1, 1)
        pulled = coef_of(1, t) * up + coef_of(2, t) * down
        pulled = pulled + coef_of(3, t) * left + coef_of(4, t) * right
        image = coef_of(0, t) * here - pulled
        q_ref[at(t), :] = image
        return dot + here * image

    for sweep in range(ITERS - 1):
        step = jnp.broadcast_to(rr / total(every(image_of, zero)), (8, LANES))

        def advance(t, norm):
            left_over = r_ref[at(t), :] - step * q_ref[at(t), :]
            r_ref[at(t), :] = left_over
            return norm + left_over * left_over

        new = total(every(advance, zero))
        ratio = jnp.broadcast_to(new / rr, (8, LANES))
        rr = new

        def turn(t, carry):
            values = p_ref[at(t), :]
            gain = step * values
            x_ref[at(t), :] = gain if sweep == 0 else x_ref[at(t), :] + gain
            direct(t, r_ref[at(t), :] + ratio * values)
            return carry

        every(turn, 0)

    step = jnp.broadcast_to(rr / total(every(image_of, zero)), (8, LANES))
    device = lax.axis_index("row") * grid_cols + lax.axis_index("col")
    mine = x_ref[at(device), :] + step * p_ref[at(device), :]
    mine = pltpu.roll(mine, 32 * lax.axis_index("row") % LANES, 1)
    groups = u_ref.shape[0] // 8 - 1
    placed = jnp.concatenate([jnp.where(lane // 8 == i, mine, 0.0) for i in range(groups)], axis=0)
    u_ref[0 : 8 * groups] = dot01([placed], widen_ref[...])
    copies = []
    for k in range(RHS):
        for i in range(groups):
            coarse = u_ref[pl.ds(8 * i + k, 8, stride=0), :]
            for part in range(HALO // 8):
                rows = pl.ds(HALO * i + 8 * part, 8)
                done_ref[k, rows, :] = base_ref[k, rows, :] + coarse
        copy = pltpu.make_async_copy(done_ref.at[k], out_ref.at[k], sem_ref.at[k])
        copy.start()
        copies.append(copy)
    for copy in copies:
        copy.wait()


def exchanged(first, second, axis, other):
    sizes = {name: lax.axis_size(name) for name in (axis, other)}

    def pairs(step):
        found = []
        for i in range(sizes["row"]):
            for j in range(sizes["col"]):
                place = {"row": i, "col": j}
                target = dict(place)
                at = place[axis]
                if step == 0:
                    target[axis] = at ^ 1
                elif at in (0, sizes[axis] - 1):
                    target[other] = place[other] ^ 1
                else:
                    target[axis] = at + 1 if at % 2 else at - 1
                found.append((i * sizes["col"] + j, target["row"] * sizes["col"] + target["col"]))
        return found

    return [lax.ppermute(part, ("row", "col"), pairs(step)) for step, part in enumerate((first, second))]


def shards(resistance, ground, nodata, patch_ids):
    grid = (lax.axis_size("row"), lax.axis_size("col"))
    devices = grid[0] * grid[1]
    rows, cols = resistance.shape
    own = [pltpu.with_memory_space_constraint(part, pltpu.HBM) for part in (resistance, ground, nodata, patch_ids)]
    def near(value):
        return pltpu.with_memory_space_constraint(value, pltpu.VMEM)

    def call(kernel, outs, scratch, *args, **options):
        outs = tuple(pltpu.VMEM(out, F32) if isinstance(out, tuple) else out for out in outs)
        scratch = [pltpu.VMEM(part, F32) if isinstance(part, tuple) else part for part in scratch]
        name = kernel.__name__
        params = pltpu.CompilerParams(vmem_limit_bytes=VMEM_LIMIT)
        return pl.pallas_call(
            kernel, out_shape=outs, scratch_shapes=scratch, name=name, compiler_params=params, **options
        )(*args)

    def all_near(values):
        return [near(value) for value in values]

    strip = (4 * HALO, cols)
    hbm = [pl.BlockSpec(memory_space=pltpu.HBM)] * 4
    near_whole = pltpu.VMEM((4, HALO, cols), jnp.int32)
    first, second = call(
        pack_rows_kernel,
        [strip, strip],
        [(4, HALO, cols), near_whole, pltpu.SemaphoreType.DMA((8,))],
        *own,
        in_specs=hbm,
    )
    tall_rows = rows + 2 * HALO
    n1 = tall_rows // 2
    tall, first_cols, second_cols, *tables = all_near(
        call(
            prepare_kernel,
            [(4, tall_rows, cols), (n1, LANES), (n1, LANES)]
            + [pltpu.VMEM((PIECES * LANES * len(tests), LANES), BF16) for tests in TABLES],
            [pltpu.VMEM((rows, cols), jnp.int32)] * 2 + [pltpu.SemaphoreType.DMA((4,))],
            *own,
            near(first),
            in_specs=hbm + [pl.BlockSpec(memory_space=pltpu.VMEM)],
            cost_estimate=pl.CostEstimate(flops=10**8, bytes_accessed=10**6, transcendentals=0),
        )
    )
    first, second = exchanged(first, second, "row", "col")
    tall, first, second = call(
        pack_cols_kernel,
        [(4, tall_rows, cols), (n1, LANES), (n1, LANES)],
        [],
        near(first),
        near(second),
        tall,
        first_cols,
        second_cols,
        input_output_aliases={2: 0, 3: 1, 4: 2},
    )
    tall = near(tall)
    first, second = exchanged(first, second, "col", "row")
    sizes = [128, 64, 32]
    inner = call(
        inner_kernel,
        [(RHS - 1, n1, LANES), (3, n1, LANES), (2, rows // 2, LANES), (4, tall_rows, LANES), (2, n1, LANES)],
        [],
        tall,
        *tables[:3],
        cost_estimate=pl.CostEstimate(flops=10**8, bytes_accessed=10**6, transcendentals=0),
    )
    payload, w0, *levels = call(
        down_kernel,
        [(devices, 8, LANES), (2, rows // 2, LANES)]
        + [(RHS - 1, size, LANES) for size in sizes]
        + [(2, size // 2, LANES) for size in sizes],
        [(4, tall_rows, LANES)] + [(3, size, LANES) for size in sizes],
        *all_near((first, second, *inner)),
        *tables[3:13],
    )
    everything = lax.all_to_all(payload, ("row", "col"), 0, 0)
    (base,) = call(
        up_kernel,
        [(RHS, rows, cols)],
        [(RHS - 1, size, LANES) for size in sizes[::-1]],
        tall,
        *all_near([w0] + levels),
        *tables[13:15],
        cost_estimate=pl.CostEstimate(flops=10**8, bytes_accessed=10**6, transcendentals=0),
    )
    return pl.pallas_call(
        functools.partial(solve_kernel, grid),
        out_shape=jax.ShapeDtypeStruct((RHS, rows, cols), F32),
        out_specs=pl.BlockSpec(memory_space=pl.ANY),
        scratch_shapes=[pltpu.VMEM((5, devices + 8, LANES), F32)]
        + [pltpu.VMEM((devices * 8, LANES), F32)] * 6
        + [pltpu.VMEM((rows // HALO * 8 + 8, LANES), F32), pltpu.VMEM((RHS, rows, cols), F32)]
        + [pltpu.SemaphoreType.DMA((RHS,))],
        compiler_params=pltpu.CompilerParams(vmem_limit_bytes=VMEM_LIMIT),
        name="solve_kernel",
    )(near(everything.reshape(devices * 8, LANES)), near(base), tables[15])


def solution(mesh):
    spec = P("row", "col")
    return jax.shard_map(shards, mesh=mesh, in_specs=(spec,) * 4, out_specs=P(None, "row", "col"), check_vma=False)
```
